32 devices in a mesh: dp: 4 (over z), ctx: 4 (over x, core), uly: 2 (over y).
Axes of the slice: x: 2, y: 2, z: 4, core: 2. Of those that a mesh axis runs over, the one named last changes fastest.
Arguments:
- queries: bfloat16 [4096, 4096], P(('dp', 'ctx', 'uly')), parts along dimension 0, may hold values from -130 to 130
- keys: bfloat16 [4096, 1024], P(('dp', 'ctx', 'uly')), parts along dimension 0, may hold values from -6.5 to 6.5
- values: bfloat16 [4096, 1024], P(('dp', 'ctx', 'uly')), parts along dimension 0, may hold values from -6 to 6
- d_out: bfloat16 [4096, 4096], P(('dp', 'ctx', 'uly')), parts along dimension 0, may hold values from -96 to 96
- rand_blocks: int32 [32, 3], P('dp'), parts along dimension 0, may hold values from 0 to 7, as said below
Outputs:
- d_queries: bfloat16 [4096, 4096], P(('dp', 'ctx', 'uly')), parts along dimension 0
- d_keys: bfloat16 [4096, 1024], P(('dp', 'ctx', 'uly')), parts along dimension 0
- d_values: bfloat16 [4096, 1024], P(('dp', 'ctx', 'uly')), parts along dimension 0
The draws below stay inside these ranges and needn't reach their ends.
There are 4 independent parts, one for each index of `dp`. The reference program is written for one: setup_inputs(seed, part) draws one part's arguments, and reference() takes and returns one part's arrays. A program takes and returns all parts, laid end to end along the dimension named above; each array names one. Nothing has to cross between parts.
Inputs may be any that keep to these rules, and one draw needn't show every extreme that they name: `rand_blocks`: for every group of 2 consecutive query blocks, the entries of its lists (window, random) that name blocks of one other group of 2 number at most 2, and at most 4 when the 2 global blocks are counted once each; both bounds are reached in every draw.
All inputs are finite; a program needn't handle non-finite values.
Results may differ from the reference program's by a relative error of at most 0.005.
Values may be sent and summed in bfloat16 or wider, within the bound.
No kernel may reach another device: no remote copies, remote signals or barrier semaphores. Data moves between devices by JAX's collectives and lax.ppermute only.
A program may use at most 128 MiB of HBM per device.

```python
import jax
import jax.numpy as jnp
from jax import lax

Q_HEADS = 32
KV_HEADS = 8
HEAD_DIM = 128
BLOCK = 128
WINDOW = 3
GLOBALS = 2
RANDOMS = 3
TOKENS = 1024
BLOCKS = 8
BLK_DEV = 2
ENTRIES = 8
GROUP = 4


def query_key_pair(key):
    base = jax.random.fold_in(key, 7)
    key_rows = jnp.clip(jax.random.normal(jax.random.fold_in(base, 1), (TOKENS, KV_HEADS, HEAD_DIM), jnp.float32), -6.0, 6.0)
    query_rows = jnp.clip(jax.random.normal(jax.random.fold_in(base, 2), (TOKENS, KV_HEADS, GROUP, HEAD_DIM), jnp.float32), -6.0, 6.0)
    return (query_rows, key_rows)


def draw_queries(key, part):
    query_rows, key_rows = query_key_pair(key)
    return query_rows.reshape(TOKENS, Q_HEADS * HEAD_DIM).astype(jnp.bfloat16)


def draw_keys(key, part):
    query_rows, key_rows = query_key_pair(key)
    return key_rows.reshape(TOKENS, KV_HEADS * HEAD_DIM).astype(jnp.bfloat16)


def draw_rand_blocks(key, part):
    groups = BLOCKS // BLK_DEV
    wanted = BLK_DEV * RANDOMS
    rounds = wanted // groups + 1
    base = jax.random.fold_in(key, 11)

    def one_group(group_index):
        group_key = jax.random.fold_in(base, group_index)
        shuffled = jnp.concatenate([jax.random.permutation(jax.random.fold_in(group_key, round_index), groups) for round_index in range(rounds)])
        last_round = jnp.arange(rounds * groups) >= (rounds - 1) * groups
        beside = (shuffled == (group_index - 1) % groups) | (shuffled == (group_index + 1) % groups)
        ranking_score = jnp.where(last_round & beside, rounds * groups, 0) + jnp.arange(rounds * groups)
        ranking = jnp.argsort(ranking_score)
        owners = shuffled[ranking[:wanted]]
        offsets = jax.random.randint(jax.random.fold_in(group_key, 1000), (wanted,), 0, BLK_DEV)
        shuffle_rows = jax.random.permutation(jax.random.fold_in(group_key, 2000), wanted)
        return (owners * BLK_DEV + offsets)[shuffle_rows].reshape(BLK_DEV, RANDOMS)
    result = jax.vmap(one_group)(jnp.arange(groups, dtype=jnp.int32))
    return result.reshape(BLOCKS, RANDOMS).astype(jnp.int32)


def level_of(rng, dims, cuts, smallest, high):
    factor_of = 1.0
    for dim, parts in cuts:
        steps = jax.random.uniform(jax.random.fold_in(jax.random.fold_in(rng, 6), dim), (parts,), jnp.float32, smallest / len(cuts), high / len(cuts))
        factor_of = factor_of * jnp.repeat(jnp.exp(steps), dims[dim] // parts).reshape((-1,) + (1,) * (len(dims) - 1 - dim))
    return factor_of


def noise(key, dims, spread, bound, cuts=(), kind=jnp.bfloat16):
    entries = spread * jax.random.normal(key, dims, jnp.float32)
    if cuts:
        entries = entries * level_of(key, dims, cuts, -0.22, 0.18)
    return jnp.clip(entries, -bound, bound).astype(kind)


def setup_inputs(seed: int = 0, part: int = 0) -> dict:
    splits = jax.random.split(jax.random.key(seed), 6)
    own_keys = jax.random.split(jax.random.fold_in(splits[5], part), 6)
    return {
        "queries": draw_queries(jax.random.fold_in(jax.random.fold_in(splits[5], part), 71), part),
        "keys": draw_keys(jax.random.fold_in(jax.random.fold_in(splits[5], part), 71), part),
        "values": noise(own_keys[2], (TOKENS, KV_HEADS * HEAD_DIM), 1.0, 6.0, ((0, 8),)),
        "d_out": noise(own_keys[3], (TOKENS, Q_HEADS * HEAD_DIM), 16.0, 96.0, ((0, 8),)),
        "rand_blocks": draw_rand_blocks(jax.random.fold_in(jax.random.fold_in(splits[5], part), 71), part),
    }


def listed_blocks(rand_blocks):
    block_ids = jnp.arange(BLOCKS, dtype=jnp.int32)
    window_part = (block_ids[:, None] + jnp.arange(WINDOW, dtype=jnp.int32)[None, :] - WINDOW // 2) % BLOCKS
    global_part = jnp.broadcast_to(jnp.arange(GLOBALS, dtype=jnp.int32)[None, :], (BLOCKS, GLOBALS))
    return jnp.concatenate([window_part, global_part, rand_blocks.astype(jnp.int32)], axis=1)


def reference(queries, keys, values, d_out, rand_blocks):
    softmax_scale = HEAD_DIM ** -0.5
    listed = listed_blocks(rand_blocks)
    query_blocks = queries.reshape(BLOCKS, BLOCK, KV_HEADS, GROUP, HEAD_DIM)
    dout_blocks = d_out.reshape(BLOCKS, BLOCK, KV_HEADS, GROUP, HEAD_DIM)
    key_blocks = keys.reshape(BLOCKS, BLOCK, KV_HEADS, HEAD_DIM)
    value_blocks = values.reshape(BLOCKS, BLOCK, KV_HEADS, HEAD_DIM)

    def one_block(carry, inputs):
        key_grads, value_grads = carry
        query_blk, dout_blk, source_rows = inputs
        query_full = query_blk.astype(jnp.float32)
        dout_full = dout_blk.astype(jnp.float32)
        key_sel = key_blocks[source_rows].astype(jnp.float32)
        value_sel = value_blocks[source_rows].astype(jnp.float32)
        scores = jnp.einsum('tkgd,eskd->kgtes', query_full, key_sel) * softmax_scale
        scores = scores.reshape(KV_HEADS, GROUP, BLOCK, ENTRIES * BLOCK)
        row_max = jnp.max(scores, axis=-1, keepdims=True)
        exp_scores = jnp.exp(scores - row_max)
        prob_rows = exp_scores / jnp.sum(exp_scores, axis=-1, keepdims=True)
        grad_probs = jnp.einsum('tkgd,eskd->kgtes', dout_full, value_sel).reshape(KV_HEADS, GROUP, BLOCK, ENTRIES * BLOCK)
        row_delta = jnp.sum(prob_rows * grad_probs, axis=-1, keepdims=True)
        grad_scores = lax.optimization_barrier((prob_rows * (grad_probs - row_delta)).astype(jnp.bfloat16)).astype(jnp.float32)
        probs_low = lax.optimization_barrier(prob_rows.astype(jnp.bfloat16)).astype(jnp.float32)
        grad_scores = grad_scores.reshape(KV_HEADS, GROUP, BLOCK, ENTRIES, BLOCK)
        probs_low = probs_low.reshape(KV_HEADS, GROUP, BLOCK, ENTRIES, BLOCK)
        grad_values = jnp.einsum('kgtes,tkgd->eskd', probs_low, dout_full)
        grad_keys = jnp.einsum('kgtes,tkgd->eskd', grad_scores, query_full) * softmax_scale
        grad_query = jnp.einsum('kgtes,eskd->tkgd', grad_scores, key_sel) * softmax_scale
        key_grads = key_grads.at[source_rows].add(grad_keys)
        value_grads = value_grads.at[source_rows].add(grad_values)
        return (key_grads, value_grads), grad_query.astype(jnp.bfloat16)

    zero_grads = jnp.zeros((BLOCKS, BLOCK, KV_HEADS, HEAD_DIM), jnp.float32)
    (key_grads, value_grads), query_grads = lax.scan(one_block, (zero_grads, zero_grads), (query_blocks, dout_blocks, listed))
    d_queries = query_grads.reshape(TOKENS, Q_HEADS * HEAD_DIM)
    d_keys = key_grads.astype(jnp.bfloat16).reshape(TOKENS, KV_HEADS * HEAD_DIM)
    d_values = value_grads.astype(jnp.bfloat16).reshape(TOKENS, KV_HEADS * HEAD_DIM)
    return (d_queries, d_keys, d_values)
```

```python
from functools import partial

import jax
import jax.numpy as jnp
from jax import lax
from jax.experimental import pallas as pl
from jax.experimental.pallas import tpu as pltpu
from jax.sharding import PartitionSpec as P

HEAD_DIM = 128
BLOCK = 128
WINDOW = 3
GLOBALS = 2
RANDOMS = 3
ENTRIES = 8
GROUP = 4


def listed_blocks(rand_blocks):
    total = rand_blocks.shape[0]
    block_ids = jnp.arange(total, dtype=jnp.int32)
    window_part = (
        block_ids[:, None] + jnp.arange(WINDOW, dtype=jnp.int32)[None, :] - WINDOW // 2
    ) % total
    global_part = jnp.broadcast_to(jnp.arange(GLOBALS, dtype=jnp.int32)[None, :], (total, GLOBALS))
    return jnp.concatenate([window_part, global_part, rand_blocks], axis=1)


def block_backward(sources, softmax_scale, inputs):
    query_blk, dout_blk, source_rows = inputs
    picked = jnp.take(sources, source_rows, axis=0)
    kv_width = picked.shape[-1] // 2
    kv_count = kv_width // HEAD_DIM
    key_sel = picked[..., :kv_width].reshape(ENTRIES, BLOCK, kv_count, HEAD_DIM)
    value_sel = picked[..., kv_width:].reshape(ENTRIES, BLOCK, kv_count, HEAD_DIM)
    query_four = query_blk.reshape(BLOCK, kv_count, GROUP, HEAD_DIM)
    dout_four = dout_blk.reshape(BLOCK, kv_count, GROUP, HEAD_DIM)
    scores = jnp.einsum("tkgd,eskd->kgtes", query_four, key_sel, preferred_element_type=jnp.float32)
    scores = scores.reshape(kv_count, GROUP, BLOCK, ENTRIES * BLOCK) * softmax_scale
    row_max = jnp.max(scores, axis=-1, keepdims=True)
    exp_scores = jnp.exp(scores - row_max)
    prob_rows = exp_scores / jnp.sum(exp_scores, axis=-1, keepdims=True)
    grad_probs = jnp.einsum(
        "tkgd,eskd->kgtes", dout_four, value_sel, preferred_element_type=jnp.float32
    )
    grad_probs = grad_probs.reshape(kv_count, GROUP, BLOCK, ENTRIES * BLOCK)
    row_delta = jnp.sum(prob_rows * grad_probs, axis=-1, keepdims=True)
    grad_scores = (
        (prob_rows * (grad_probs - row_delta))
        .astype(jnp.bfloat16)
        .reshape(kv_count, GROUP, BLOCK, ENTRIES, BLOCK)
    )
    probs_low = prob_rows.astype(jnp.bfloat16).reshape(kv_count, GROUP, BLOCK, ENTRIES, BLOCK)
    grad_values = jnp.einsum(
        "kgtes,tkgd->eskd", probs_low, dout_four, preferred_element_type=jnp.float32
    )
    grad_keys = (
        jnp.einsum("kgtes,tkgd->eskd", grad_scores, query_four, preferred_element_type=jnp.float32)
        * softmax_scale
    )
    grad_query = (
        jnp.einsum("kgtes,eskd->tkgd", grad_scores, key_sel, preferred_element_type=jnp.float32)
        * softmax_scale
    )
    partials = jnp.concatenate(
        [
            grad_keys.reshape(ENTRIES, BLOCK, kv_width),
            grad_values.reshape(ENTRIES, BLOCK, kv_width),
        ],
        axis=-1,
    )
    return (partials, grad_query.reshape(BLOCK, kv_count * GROUP * HEAD_DIM))


def per_device_sparse(queries, keys, values, d_out, rand_blocks):
    softmax_scale = HEAD_DIM ** (-0.5)
    groups = lax.axis_size("ctx")
    my_group = lax.axis_index("ctx")
    queries_here, dout_here, keys_here, values_here = (
        lax.all_to_all(queries, "uly", split_axis=1, concat_axis=0, tiled=True),
        lax.all_to_all(d_out, "uly", split_axis=1, concat_axis=0, tiled=True),
        lax.all_to_all(keys, "uly", split_axis=1, concat_axis=0, tiled=True),
        lax.all_to_all(values, "uly", split_axis=1, concat_axis=0, tiled=True),
    )
    tokens_here = keys_here.shape[0]
    per_group = tokens_here // BLOCK
    kv_width = keys_here.shape[1]
    local_blocks = jnp.concatenate([keys_here, values_here], axis=1).reshape(
        per_group, BLOCK, 2 * kv_width
    )
    listed = listed_blocks(rand_blocks)
    owners = listed // per_group
    offsets = listed % per_group
    requester = (jnp.arange(listed.shape[0], dtype=jnp.int32) // per_group)[:, None]
    entry_ids = jnp.arange(ENTRIES, dtype=jnp.int32)
    is_global = (entry_ids >= WINDOW) & (entry_ids < WINDOW + GLOBALS)
    entry_global = jnp.tile(is_global, per_group)
    global_slot = jnp.tile(entry_ids - WINDOW, per_group)
    rand_capacity = per_group * RANDOMS // groups + 1
    remote = owners != requester
    capacity = rand_capacity + GLOBALS
    lead_slots = GLOBALS
    owners = owners.reshape(groups, per_group * ENTRIES)
    offsets = offsets.reshape(groups, per_group * ENTRIES)
    remote = remote.reshape(groups, per_group * ENTRIES)
    counted = remote & jnp.logical_not(entry_global)[None, :]
    owner_hot = (
        (owners[:, :, None] == jnp.arange(groups, dtype=jnp.int32)[None, None, :])
        & counted[:, :, None]
    ).astype(jnp.int32)
    rand_slot = jnp.sum((jnp.cumsum(owner_hot, axis=1) - 1) * owner_hot, axis=2) + lead_slots
    slot_index = jnp.where(entry_global[None, :], global_slot[None, :], rand_slot)
    for_me = remote & (owners == my_group)
    slot_match = (
        slot_index[:, :, None, None] == jnp.arange(capacity, dtype=jnp.int32)[None, None, :, None]
    )
    block_match = (
        offsets[:, :, None, None] == jnp.arange(per_group, dtype=jnp.int32)[None, None, None, :]
    )
    slot_picker = jnp.minimum(
        jnp.sum((for_me[:, :, None, None] & slot_match & block_match).astype(jnp.int32), axis=1), 1
    )
    outgoing = jnp.einsum(
        "csb,bxd->csxd",
        slot_picker.astype(jnp.bfloat16),
        local_blocks,
        preferred_element_type=jnp.float32,
    ).astype(jnp.bfloat16)
    incoming = lax.all_to_all(outgoing, "ctx", split_axis=0, concat_axis=0, tiled=True)
    my_owner = lax.dynamic_index_in_dim(owners, my_group, 0, keepdims=False)
    my_slot = lax.dynamic_index_in_dim(slot_index, my_group, 0, keepdims=False)
    my_offset = lax.dynamic_index_in_dim(offsets, my_group, 0, keepdims=False)
    my_remote = lax.dynamic_index_in_dim(remote, my_group, 0, keepdims=False)
    source_rows = jnp.where(my_remote, per_group + my_owner * capacity + my_slot, my_offset)
    pieces = [local_blocks, incoming.reshape(groups * capacity, BLOCK, 2 * kv_width)]
    sources = jnp.concatenate(pieces, axis=0)
    source_count = sources.shape[0]
    query_blocks = queries_here.reshape(per_group, BLOCK, queries_here.shape[1])
    dout_blocks = dout_here.reshape(per_group, BLOCK, dout_here.shape[1])
    partials, grad_query = lax.map(
        partial(block_backward, sources, softmax_scale),
        (query_blocks, dout_blocks, source_rows.reshape(per_group, ENTRIES)),
    )
    source_hot = (
        source_rows[:, None] == jnp.arange(source_count, dtype=jnp.int32)[None, :]
    ).astype(jnp.float32)
    source_grads = jnp.einsum(
        "ms,mxd->sxd",
        source_hot,
        partials.reshape(per_group * ENTRIES, BLOCK, 2 * kv_width),
        precision=lax.Precision.HIGHEST,
    )
    own_grads = source_grads[:per_group]
    sent_grads = source_grads[per_group : per_group + groups * capacity].reshape(
        groups, capacity, BLOCK, 2 * kv_width
    )
    returned = lax.all_to_all(sent_grads, "ctx", split_axis=0, concat_axis=0, tiled=True)
    own_grads = own_grads + jnp.einsum(
        "csb,csxd->bxd", slot_picker.astype(jnp.float32), returned, precision=lax.Precision.HIGHEST
    )
    query_grads = grad_query.reshape(tokens_here, queries_here.shape[1]).astype(jnp.bfloat16)
    key_grads = own_grads[..., :kv_width].reshape(tokens_here, kv_width).astype(jnp.bfloat16)
    value_grads = own_grads[..., kv_width:].reshape(tokens_here, kv_width).astype(jnp.bfloat16)
    d_queries, d_keys, d_values = (
        lax.all_to_all(query_grads, "uly", split_axis=0, concat_axis=1, tiled=True),
        lax.all_to_all(key_grads, "uly", split_axis=0, concat_axis=1, tiled=True),
        lax.all_to_all(value_grads, "uly", split_axis=0, concat_axis=1, tiled=True),
    )
    return (d_queries, d_keys, d_values)


LOG2E = 1.4426950408889634
PART = 8
HEAD_HALF = 4
CHUNKS = 1
HALF_Q = HEAD_HALF * GROUP * HEAD_DIM
HALF_KV = HEAD_HALF * HEAD_DIM
PAIR = 2 * BLOCK
AXES = ("ctx", "uly")

SWAP = 2


def perm_to(first, second):
    return [(i, i ^ (second if i & SWAP else first)) for i in range(PART)]


SWAP_PERM = perm_to(SWAP, SWAP)
NEAR_PERM = perm_to(4, 1)
FAR_PERM = perm_to(1, 4)


def send(array, perm):
    return lax.ppermute(array, AXES, perm)


def pack_kernel(chunks, where_ref, k_ref, v_ref, ko_ref, vo_ref, *outs):
    heads = HEAD_HALF // chunks
    for chunk in range(chunks):
        for head in range(heads):
            src = slice((chunk * heads + head) * HEAD_DIM, (chunk * heads + head + 1) * HEAD_DIM)
            for side, ref in enumerate((k_ref, v_ref)):
                cols = slice((2 * head + side) * HEAD_DIM, (2 * head + side + 1) * HEAD_DIM)
                outs[chunk][0:BLOCK, cols] = ref[:, src]
            for side, ref in enumerate((ko_ref, vo_ref)):
                cols = slice((2 * head + side) * HEAD_DIM, (2 * head + side + 1) * HEAD_DIM)
                outs[chunk][BLOCK:PAIR, cols] = ref[:, src]


def pack_pairs(where, keys, values, keys_other, values_other):
    width = 2 * HALF_KV // CHUNKS
    spec = pl.BlockSpec((BLOCK, HALF_KV), lambda g, w: (0, w[0]))
    return pl.pallas_call(
        partial(pack_kernel, CHUNKS),
        out_shape=[jax.ShapeDtypeStruct((PAIR, width), jnp.bfloat16)] * CHUNKS,
        grid_spec=pltpu.PrefetchScalarGridSpec(
            num_scalar_prefetch=1,
            grid=(1,),
            in_specs=[spec] * 4,
            out_specs=[pl.BlockSpec((PAIR, width), lambda g, w: (0, 0))] * CHUNKS,
        ),
        name="pack_pairs",
        cost_estimate=pl.CostEstimate(flops=0, bytes_accessed=2**20, transcendentals=0),
    )(where, keys, values, keys_other, values_other)


def attend_kernel(
    where_ref,
    rand_ref,
    q_ref,
    do_ref,
    qo_ref,
    doo_ref,
    pair_ref,
    near_ref,
    far_ref,
    corner_ref,
    dq_ref,
    dqo_ref,
    own_out,
    near_out,
    far_out,
    corner_out,
    s_ref,
    dp_ref,
    qcat_ref,
    docat_ref,
    dk_ref,
    dv_ref,
):
    scale = HEAD_DIM ** (-0.5)
    step = pl.program_id(1)
    half = where_ref[0]
    me = where_ref[1]
    near = 4 - 3 * half
    far = 1 + 3 * half
    block = me ^ (SWAP * step)
    mine = step == 0
    sources = (pair_ref, near_ref, far_ref, corner_ref)
    deltas = (0, near, far, near ^ far)

    @pl.when(mine)
    def _():
        for g in range(GROUP):
            qcat_ref[g * BLOCK : (g + 1) * BLOCK, :] = q_ref[:, g * HEAD_DIM : (g + 1) * HEAD_DIM]
            docat_ref[g * BLOCK : (g + 1) * BLOCK, :] = do_ref[:, g * HEAD_DIM : (g + 1) * HEAD_DIM]
        dk_ref[...] = jnp.zeros_like(dk_ref)
        dv_ref[...] = jnp.zeros_like(dv_ref)

    @pl.when(jnp.logical_not(mine))
    def _():
        for g in range(GROUP):
            qcat_ref[g * BLOCK : (g + 1) * BLOCK, :] = qo_ref[:, g * HEAD_DIM : (g + 1) * HEAD_DIM]
            docat_ref[g * BLOCK : (g + 1) * BLOCK, :] = doo_ref[
                :, g * HEAD_DIM : (g + 1) * HEAD_DIM
            ]

    def count_of(slot):
        listed = me ^ deltas[slot // 2] ^ (SWAP * (slot % 2))
        total = jnp.int32(0)
        for w in range(WINDOW):
            total += (lax.rem(block + (w - WINDOW // 2 + PART), PART) == listed).astype(jnp.int32)
        total += (listed < GLOBALS).astype(jnp.int32)
        for r in range(RANDOMS):
            total += (rand_ref[block * RANDOMS + r] == listed).astype(jnp.int32)
        return total

    counts = [count_of(slot) for slot in range(PART)]
    qcat = qcat_ref[...]
    docat = docat_ref[...]
    rows = GROUP * BLOCK
    contract_last = (((1,), (1,)), ((), ()))
    contract = (((1,), (0,)), ((), ()))

    def key_of(slot):
        base = (slot % 2) * BLOCK
        return sources[slot // 2][base : base + BLOCK, 0:HEAD_DIM]

    def value_of(slot):
        base = (slot % 2) * BLOCK
        return sources[slot // 2][base : base + BLOCK, HEAD_DIM : 2 * HEAD_DIM]

    top = None
    for slot in range(PART):
        s = lax.dot_general(key_of(slot), qcat, contract_last, preferred_element_type=jnp.float32)
        s_ref[slot] = s
        part = jnp.max(s.reshape(BLOCK // 8, 8, rows), axis=0)
        part = jnp.where(counts[slot] > 0, part, -1e30)
        top = part if top is None else jnp.maximum(top, part)
        dp_ref[slot] = lax.dot_general(
            value_of(slot), docat, contract_last, preferred_element_type=jnp.float32
        )
    factor = scale * LOG2E
    top = jnp.max(top, axis=0, keepdims=True) * factor
    total = jnp.zeros((8, rows), jnp.float32)
    delta = jnp.zeros((8, rows), jnp.float32)
    for slot in range(PART):
        shift = jnp.where(counts[slot] > 0, top, 1e30)
        weight = counts[slot].astype(jnp.float32)
        e = jnp.exp2(s_ref[slot] * factor - shift)
        s_ref[slot] = e
        total += weight * jnp.sum(e.reshape(BLOCK // 8, 8, rows), axis=0)
        delta += weight * jnp.sum((e * dp_ref[slot]).reshape(BLOCK // 8, 8, rows), axis=0)
    inverse = 1.0 / jnp.sum(total, axis=0, keepdims=True)
    delta = jnp.sum(delta, axis=0, keepdims=True) * inverse
    dq = None
    for slot in range(PART):
        p = s_ref[slot] * (counts[slot].astype(jnp.float32) * inverse)
        ds = (p * (dp_ref[slot] - delta)).astype(jnp.bfloat16)
        dv_ref[slot] += lax.dot_general(
            p.astype(jnp.bfloat16), docat, contract, preferred_element_type=jnp.float32
        )
        dk_ref[slot] += lax.dot_general(ds, qcat, contract, preferred_element_type=jnp.float32)
        term = lax.dot_general(
            key_of(slot).T, ds, contract, preferred_element_type=jnp.float32
        )
        dq = term if dq is None else dq + term
    dq = (dq * scale).T.astype(jnp.bfloat16)

    @pl.when(mine)
    def _():
        for g in range(GROUP):
            dq_ref[:, g * HEAD_DIM : (g + 1) * HEAD_DIM] = dq[g * BLOCK : (g + 1) * BLOCK]

    @pl.when(jnp.logical_not(mine))
    def _():
        for g in range(GROUP):
            dqo_ref[:, g * HEAD_DIM : (g + 1) * HEAD_DIM] = dq[g * BLOCK : (g + 1) * BLOCK]
        for place, out in enumerate((own_out, near_out, far_out, corner_out)):
            for r in range(2):
                base = slice(r * BLOCK, (r + 1) * BLOCK)
                out[base, 0:HEAD_DIM] = (dk_ref[2 * place + r] * scale).astype(out.dtype)
                out[base, HEAD_DIM : 2 * HEAD_DIM] = dv_ref[2 * place + r].astype(out.dtype)


def attend(chunk, where, rand, queries, d_out, queries_other, dout_other, sources):
    heads = HEAD_HALF // CHUNKS
    qw = GROUP * HEAD_DIM
    kw = 2 * HEAD_DIM
    first = chunk * heads
    q_spec = pl.BlockSpec((BLOCK, qw), lambda j, b, w, r: (0, w[0] * HEAD_HALF + first + j))
    kv_spec = pl.BlockSpec((PAIR, kw), lambda j, b, w, r: (0, j))
    dq_spec = pl.BlockSpec((BLOCK, qw), lambda j, b, w, r: (0, j))
    rows = GROUP * BLOCK
    pairs = 2 * heads * rows * PART * BLOCK
    dq_shape = jax.ShapeDtypeStruct((BLOCK, heads * qw), jnp.bfloat16)
    wide = jax.ShapeDtypeStruct((PAIR, heads * kw), jnp.float32)
    narrow = jax.ShapeDtypeStruct((PAIR, heads * kw), jnp.bfloat16)
    return pl.pallas_call(
        attend_kernel,
        out_shape=[dq_shape, dq_shape, wide, wide, narrow, narrow],
        grid_spec=pltpu.PrefetchScalarGridSpec(
            num_scalar_prefetch=2,
            grid=(heads, 2),
            in_specs=[q_spec] * 4 + [kv_spec] * 4,
            out_specs=[dq_spec] * 2 + [kv_spec] * 4,
            scratch_shapes=[
                pltpu.VMEM((PART, BLOCK, rows), jnp.float32),
                pltpu.VMEM((PART, BLOCK, rows), jnp.float32),
                pltpu.VMEM((rows, HEAD_DIM), jnp.bfloat16),
                pltpu.VMEM((rows, HEAD_DIM), jnp.bfloat16),
                pltpu.VMEM((PART, BLOCK, HEAD_DIM), jnp.float32),
                pltpu.VMEM((PART, BLOCK, HEAD_DIM), jnp.float32),
            ],
        ),
        name="attend",
        compiler_params=pltpu.CompilerParams(vmem_limit_bytes=24 * 2**20),
        cost_estimate=pl.CostEstimate(
            flops=10 * pairs * HEAD_DIM * 2, bytes_accessed=4 * 2**20, transcendentals=pairs
        ),
    )(where, rand, queries, d_out, queries_other, dout_other, *sources)


def finish_kernel(chunks, where_ref, *refs):
    heads = HEAD_HALF // chunks
    own, other, dq_own, dq_got = (refs[i * chunks : (i + 1) * chunks] for i in range(4))
    dq_ref, dk_ref, dv_ref = refs[4 * chunks :]
    half = where_ref[0]
    for value in range(2):

        @pl.when(half == value)
        def _():
            for piece, place in ((own, value), (other, 1 - value)):
                for chunk in range(chunks):
                    for head in range(heads):
                        at = place * HALF_KV + (chunk * heads + head) * HEAD_DIM
                        from_col = 2 * head * HEAD_DIM
                        dk_ref[:, at : at + HEAD_DIM] = piece[chunk][
                            0:BLOCK, from_col : from_col + HEAD_DIM
                        ]
                        dv_ref[:, at : at + HEAD_DIM] = piece[chunk][
                            0:BLOCK, from_col + HEAD_DIM : from_col + 2 * HEAD_DIM
                        ]
            width = HALF_Q // chunks
            for piece, place in ((dq_own, value), (dq_got, 1 - value)):
                for chunk in range(chunks):
                    at = place * HALF_Q + chunk * width
                    dq_ref[:, at : at + width] = piece[chunk][...]


def finish(where, own, other, dq_own, dq_got):
    return pl.pallas_call(
        partial(finish_kernel, CHUNKS),
        out_shape=[
            jax.ShapeDtypeStruct((BLOCK, 2 * HALF_Q), jnp.bfloat16),
            jax.ShapeDtypeStruct((BLOCK, 2 * HALF_KV), jnp.bfloat16),
            jax.ShapeDtypeStruct((BLOCK, 2 * HALF_KV), jnp.bfloat16),
        ],
        in_specs=[pl.BlockSpec(memory_space=pltpu.SMEM)]
        + [pl.BlockSpec(memory_space=pltpu.VMEM)] * (4 * CHUNKS),
        out_specs=[pl.BlockSpec(memory_space=pltpu.VMEM)] * 3,
        name="finish",
        cost_estimate=pl.CostEstimate(flops=0, bytes_accessed=3 * 2**20, transcendentals=0),
    )(where, *own, *other, *dq_own, *dq_got)


def per_device_dense(queries, keys, values, d_out, rand_blocks):
    me = lax.axis_index("ctx") * 2 + lax.axis_index("uly")
    half = lax.axis_index("ctx") % 2
    where = jnp.stack([half, me]).astype(jnp.int32)
    rand = rand_blocks.reshape(PART * RANDOMS)
    keys_other = send(keys, SWAP_PERM)
    values_other = send(values, SWAP_PERM)
    queries_other = send(queries, SWAP_PERM)
    dout_other = send(d_out, SWAP_PERM)
    pairs = pack_pairs(where, keys, values, keys_other, values_other)
    nears = [send(pair, NEAR_PERM) for pair in pairs]
    fars = [send(pair, FAR_PERM) for pair in pairs]
    corners = [send(near, FAR_PERM) for near in nears]
    own, other, dq_own, dq_got = [], [], [], []
    for chunk in range(CHUNKS):
        dq_mine, dq_other, own_grads, near_grads, far_grads, corner_grads = attend(
            chunk,
            where,
            rand,
            queries,
            d_out,
            queries_other,
            dout_other,
            (pairs[chunk], nears[chunk], fars[chunk], corners[chunk]),
        )
        from_corner = send(corner_grads, FAR_PERM)
        from_far = send(far_grads, FAR_PERM)
        relayed = (near_grads + from_corner.astype(jnp.float32)).astype(jnp.bfloat16)
        from_near = send(relayed, NEAR_PERM)
        total = own_grads + from_far.astype(jnp.float32) + from_near.astype(jnp.float32)
        total = total.astype(jnp.bfloat16)
        own.append(total[:BLOCK])
        other.append(send(total[BLOCK:], SWAP_PERM))
        dq_own.append(dq_mine)
        dq_got.append(send(dq_other, SWAP_PERM))
    return tuple(finish(where, own, other, dq_own, dq_got))


def per_device(queries, keys, values, d_out, rand_blocks):
    dense = (
        lax.axis_size("ctx") == 4
        and lax.axis_size("uly") == 2
        and rand_blocks.shape[0] == PART
        and keys.shape == (BLOCK, 2 * HALF_KV)
    )
    plan = per_device_dense if dense else per_device_sparse
    return plan(queries, keys, values, d_out, rand_blocks)


def solution(mesh):
    in_specs = (
        P(("dp", "ctx", "uly"), None),
        P(("dp", "ctx", "uly"), None),
        P(("dp", "ctx", "uly"), None),
        P(("dp", "ctx", "uly"), None),
        P("dp", None),
    )
    out_specs = (
        P(("dp", "ctx", "uly"), None),
        P(("dp", "ctx", "uly"), None),
        P(("dp", "ctx", "uly"), None),
    )
    return jax.shard_map(
        per_device, mesh=mesh, in_specs=in_specs, out_specs=out_specs, check_vma=False
    )
```

```python
from functools import partial

import jax
import jax.numpy as jnp
from jax import lax
from jax.experimental import pallas as pl
from jax.experimental.pallas import tpu as pltpu
from jax.sharding import PartitionSpec as P

HEAD_DIM = 128
BLOCK = 128
WINDOW = 3
GLOBALS = 2
RANDOMS = 3
ENTRIES = 8
GROUP = 4


def listed_blocks(rand_blocks):
    total = rand_blocks.shape[0]
    block_ids = jnp.arange(total, dtype=jnp.int32)
    window_part = (
        block_ids[:, None] + jnp.arange(WINDOW, dtype=jnp.int32)[None, :] - WINDOW // 2
    ) % total
    global_part = jnp.broadcast_to(jnp.arange(GLOBALS, dtype=jnp.int32)[None, :], (total, GLOBALS))
    return jnp.concatenate([window_part, global_part, rand_blocks], axis=1)


def block_backward(sources, softmax_scale, inputs):
    query_blk, dout_blk, source_rows = inputs
    picked = jnp.take(sources, source_rows, axis=0)
    kv_width = picked.shape[-1] // 2
    kv_count = kv_width // HEAD_DIM
    key_sel = picked[..., :kv_width].reshape(ENTRIES, BLOCK, kv_count, HEAD_DIM)
    value_sel = picked[..., kv_width:].reshape(ENTRIES, BLOCK, kv_count, HEAD_DIM)
    query_four = query_blk.reshape(BLOCK, kv_count, GROUP, HEAD_DIM)
    dout_four = dout_blk.reshape(BLOCK, kv_count, GROUP, HEAD_DIM)
    scores = jnp.einsum("tkgd,eskd->kgtes", query_four, key_sel, preferred_element_type=jnp.float32)
    scores = scores.reshape(kv_count, GROUP, BLOCK, ENTRIES * BLOCK) * softmax_scale
    row_max = jnp.max(scores, axis=-1, keepdims=True)
    exp_scores = jnp.exp(scores - row_max)
    prob_rows = exp_scores / jnp.sum(exp_scores, axis=-1, keepdims=True)
    grad_probs = jnp.einsum(
        "tkgd,eskd->kgtes", dout_four, value_sel, preferred_element_type=jnp.float32
    )
    grad_probs = grad_probs.reshape(kv_count, GROUP, BLOCK, ENTRIES * BLOCK)
    row_delta = jnp.sum(prob_rows * grad_probs, axis=-1, keepdims=True)
    grad_scores = (
        (prob_rows * (grad_probs - row_delta))
        .astype(jnp.bfloat16)
        .reshape(kv_count, GROUP, BLOCK, ENTRIES, BLOCK)
    )
    probs_low = prob_rows.astype(jnp.bfloat16).reshape(kv_count, GROUP, BLOCK, ENTRIES, BLOCK)
    grad_values = jnp.einsum(
        "kgtes,tkgd->eskd", probs_low, dout_four, preferred_element_type=jnp.float32
    )
    grad_keys = (
        jnp.einsum("kgtes,tkgd->eskd", grad_scores, query_four, preferred_element_type=jnp.float32)
        * softmax_scale
    )
    grad_query = (
        jnp.einsum("kgtes,eskd->tkgd", grad_scores, key_sel, preferred_element_type=jnp.float32)
        * softmax_scale
    )
    partials = jnp.concatenate(
        [
            grad_keys.reshape(ENTRIES, BLOCK, kv_width),
            grad_values.reshape(ENTRIES, BLOCK, kv_width),
        ],
        axis=-1,
    )
    return (partials, grad_query.reshape(BLOCK, kv_count * GROUP * HEAD_DIM))


def per_device_sparse(queries, keys, values, d_out, rand_blocks):
    softmax_scale = HEAD_DIM ** (-0.5)
    groups = lax.axis_size("ctx")
    my_group = lax.axis_index("ctx")
    queries_here, dout_here, keys_here, values_here = (
        lax.all_to_all(queries, "uly", split_axis=1, concat_axis=0, tiled=True),
        lax.all_to_all(d_out, "uly", split_axis=1, concat_axis=0, tiled=True),
        lax.all_to_all(keys, "uly", split_axis=1, concat_axis=0, tiled=True),
        lax.all_to_all(values, "uly", split_axis=1, concat_axis=0, tiled=True),
    )
    tokens_here = keys_here.shape[0]
    per_group = tokens_here // BLOCK
    kv_width = keys_here.shape[1]
    local_blocks = jnp.concatenate([keys_here, values_here], axis=1).reshape(
        per_group, BLOCK, 2 * kv_width
    )
    listed = listed_blocks(rand_blocks)
    owners = listed // per_group
    offsets = listed % per_group
    requester = (jnp.arange(listed.shape[0], dtype=jnp.int32) // per_group)[:, None]
    entry_ids = jnp.arange(ENTRIES, dtype=jnp.int32)
    is_global = (entry_ids >= WINDOW) & (entry_ids < WINDOW + GLOBALS)
    entry_global = jnp.tile(is_global, per_group)
    global_slot = jnp.tile(entry_ids - WINDOW, per_group)
    rand_capacity = per_group * RANDOMS // groups + 1
    remote = owners != requester
    capacity = rand_capacity + GLOBALS
    lead_slots = GLOBALS
    owners = owners.reshape(groups, per_group * ENTRIES)
    offsets = offsets.reshape(groups, per_group * ENTRIES)
    remote = remote.reshape(groups, per_group * ENTRIES)
    counted = remote & jnp.logical_not(entry_global)[None, :]
    owner_hot = (
        (owners[:, :, None] == jnp.arange(groups, dtype=jnp.int32)[None, None, :])
        & counted[:, :, None]
    ).astype(jnp.int32)
    rand_slot = jnp.sum((jnp.cumsum(owner_hot, axis=1) - 1) * owner_hot, axis=2) + lead_slots
    slot_index = jnp.where(entry_global[None, :], global_slot[None, :], rand_slot)
    for_me = remote & (owners == my_group)
    slot_match = (
        slot_index[:, :, None, None] == jnp.arange(capacity, dtype=jnp.int32)[None, None, :, None]
    )
    block_match = (
        offsets[:, :, None, None] == jnp.arange(per_group, dtype=jnp.int32)[None, None, None, :]
    )
    slot_picker = jnp.minimum(
        jnp.sum((for_me[:, :, None, None] & slot_match & block_match).astype(jnp.int32), axis=1), 1
    )
    outgoing = jnp.einsum(
        "csb,bxd->csxd",
        slot_picker.astype(jnp.bfloat16),
        local_blocks,
        preferred_element_type=jnp.float32,
    ).astype(jnp.bfloat16)
    incoming = lax.all_to_all(outgoing, "ctx", split_axis=0, concat_axis=0, tiled=True)
    my_owner = lax.dynamic_index_in_dim(owners, my_group, 0, keepdims=False)
    my_slot = lax.dynamic_index_in_dim(slot_index, my_group, 0, keepdims=False)
    my_offset = lax.dynamic_index_in_dim(offsets, my_group, 0, keepdims=False)
    my_remote = lax.dynamic_index_in_dim(remote, my_group, 0, keepdims=False)
    source_rows = jnp.where(my_remote, per_group + my_owner * capacity + my_slot, my_offset)
    pieces = [local_blocks, incoming.reshape(groups * capacity, BLOCK, 2 * kv_width)]
    sources = jnp.concatenate(pieces, axis=0)
    source_count = sources.shape[0]
    query_blocks = queries_here.reshape(per_group, BLOCK, queries_here.shape[1])
    dout_blocks = dout_here.reshape(per_group, BLOCK, dout_here.shape[1])
    partials, grad_query = lax.map(
        partial(block_backward, sources, softmax_scale),
        (query_blocks, dout_blocks, source_rows.reshape(per_group, ENTRIES)),
    )
    source_hot = (
        source_rows[:, None] == jnp.arange(source_count, dtype=jnp.int32)[None, :]
    ).astype(jnp.float32)
    source_grads = jnp.einsum(
        "ms,mxd->sxd",
        source_hot,
        partials.reshape(per_group * ENTRIES, BLOCK, 2 * kv_width),
        precision=lax.Precision.HIGHEST,
    )
    own_grads = source_grads[:per_group]
    sent_grads = source_grads[per_group : per_group + groups * capacity].reshape(
        groups, capacity, BLOCK, 2 * kv_width
    )
    returned = lax.all_to_all(sent_grads, "ctx", split_axis=0, concat_axis=0, tiled=True)
    own_grads = own_grads + jnp.einsum(
        "csb,csxd->bxd", slot_picker.astype(jnp.float32), returned, precision=lax.Precision.HIGHEST
    )
    query_grads = grad_query.reshape(tokens_here, queries_here.shape[1]).astype(jnp.bfloat16)
    key_grads = own_grads[..., :kv_width].reshape(tokens_here, kv_width).astype(jnp.bfloat16)
    value_grads = own_grads[..., kv_width:].reshape(tokens_here, kv_width).astype(jnp.bfloat16)
    d_queries, d_keys, d_values = (
        lax.all_to_all(query_grads, "uly", split_axis=0, concat_axis=1, tiled=True),
        lax.all_to_all(key_grads, "uly", split_axis=0, concat_axis=1, tiled=True),
        lax.all_to_all(value_grads, "uly", split_axis=0, concat_axis=1, tiled=True),
    )
    return (d_queries, d_keys, d_values)


LOG2E = 1.4426950408889634
PART = 8
HEAD_HALF = 4
CHUNKS = (2, 2)
DIRECT = (True, True)
VMEM_MIB = 48
HALF_Q = HEAD_HALF * GROUP * HEAD_DIM
HALF_KV = HEAD_HALF * HEAD_DIM
PAIR = 2 * BLOCK
AXES = ("ctx", "uly")

SWAP = 2


def perm_to(first, second):
    return [(i, i ^ (second if i & SWAP else first)) for i in range(PART)]


SWAP_PERM = perm_to(SWAP, SWAP)
CORNER_PERM = perm_to(5, 5)
NEAR_PERM = perm_to(4, 1)
FAR_PERM = perm_to(1, 4)


def send(array, perm):
    return lax.ppermute(array, AXES, perm)


def pack_kernel(where_ref, k_ref, v_ref, ko_ref, vo_ref, *outs):
    for chunk, heads in enumerate(CHUNKS):
        for head in range(heads):
            at = sum(CHUNKS[:chunk]) + head
            src = slice(at * HEAD_DIM, (at + 1) * HEAD_DIM)
            for side, ref in enumerate((k_ref, v_ref)):
                cols = slice((2 * head + side) * HEAD_DIM, (2 * head + side + 1) * HEAD_DIM)
                outs[chunk][0:BLOCK, cols] = ref[:, src]
            for side, ref in enumerate((ko_ref, vo_ref)):
                cols = slice((2 * head + side) * HEAD_DIM, (2 * head + side + 1) * HEAD_DIM)
                outs[chunk][BLOCK:PAIR, cols] = ref[:, src]


def pack_pairs(where, keys, values, keys_other, values_other):
    shapes = [(PAIR, 2 * HEAD_DIM * heads) for heads in CHUNKS]
    spec = pl.BlockSpec((BLOCK, HALF_KV), lambda g, w: (0, w[0]))
    return pl.pallas_call(
        pack_kernel,
        out_shape=[jax.ShapeDtypeStruct(shape, jnp.bfloat16) for shape in shapes],
        grid_spec=pltpu.PrefetchScalarGridSpec(
            num_scalar_prefetch=1,
            grid=(1,),
            in_specs=[spec] * 4,
            out_specs=[pl.BlockSpec(shape, lambda g, w: (0, 0)) for shape in shapes],
        ),
        name="pack_pairs",
        cost_estimate=pl.CostEstimate(flops=0, bytes_accessed=2**20, transcendentals=0),
    )(where, keys, values, keys_other, values_other)


def attend_kernel(
    where_ref,
    rand_ref,
    q_ref,
    do_ref,
    qo_ref,
    doo_ref,
    pair_ref,
    near_ref,
    far_ref,
    corner_ref,
    dq_ref,
    dqo_ref,
    own_out,
    near_out,
    far_out,
    corner_out,
    s_ref,
    dp_ref,
    q_rows,
    do_rows,
    k_rows,
    v_rows,
    dk_ref,
    dv_ref,
):
    scale = HEAD_DIM ** (-0.5)
    factor = scale * LOG2E
    half = where_ref[0]
    me = where_ref[1]
    near = 4 - 3 * half
    far = 1 + 3 * half
    deltas = (0, near, far, near ^ far)
    outs = (own_out, near_out, far_out, corner_out)
    dq_outs = (dq_ref, dqo_ref)
    rows = GROUP * BLOCK
    unit = rows // 2
    units = 2 * rows // unit
    span = 4 * BLOCK
    spans = PART * BLOCK // span
    last = (((1,), (1,)), ((), ()))
    plain = (((1,), (0,)), ((), ()))
    first = (((0,), (0,)), ((), ()))
    dot = partial(lax.dot_general, preferred_element_type=jnp.float32)

    for b, (q, do) in enumerate(((q_ref, do_ref), (qo_ref, doo_ref))):
        for g in range(GROUP):
            at = slice(b * rows + g * BLOCK, b * rows + (g + 1) * BLOCK)
            q_rows[at, :] = q[:, g * HEAD_DIM : (g + 1) * HEAD_DIM]
            do_rows[at, :] = do[:, g * HEAD_DIM : (g + 1) * HEAD_DIM]
    for place, source in enumerate((pair_ref, near_ref, far_ref, corner_ref)):
        at = slice(place * PAIR, (place + 1) * PAIR)
        k_rows[at, :] = source[:, 0:HEAD_DIM]
        v_rows[at, :] = source[:, HEAD_DIM : 2 * HEAD_DIM]

    def count_of(b, slot):
        block = me ^ (SWAP * b)
        listed = me ^ deltas[slot // 2] ^ (SWAP * (slot % 2))
        total = (listed < GLOBALS).astype(jnp.int32)
        for w in range(WINDOW):
            total += (lax.rem(block + (w - WINDOW // 2 + PART), PART) == listed).astype(jnp.int32)
        for r in range(RANDOMS):
            total += (rand_ref[block * RANDOMS + r] == listed).astype(jnp.int32)
        return total

    counts = [[count_of(b, slot) for slot in range(PART)] for b in range(2)]

    def slots_of(u, n):
        for i in range(span // BLOCK):
            slot = n * (span // BLOCK) + i
            yield i, slice(slot * BLOCK, (slot + 1) * BLOCK), counts[u * unit // rows][slot]

    def fold(x, op):
        return op(x.reshape(BLOCK // 8, 8, unit), axis=0)

    def cols_of(u):
        return slice(u * unit, (u + 1) * unit)

    def span_of(n):
        return slice(n * span, (n + 1) * span)

    top, sums, inverse, dq = [None] * units, [None] * units, [None] * units, [None] * units

    def score(u, n):
        s = dot(k_rows[span_of(n), :], q_rows[cols_of(u), :], last)
        s_ref[span_of(n), cols_of(u)] = s
        for i, _, count in slots_of(u, n):
            part = fold(s[i * BLOCK : (i + 1) * BLOCK], jnp.max)
            part = jnp.where(count > 0, part, -1e30)
            top[u] = part if top[u] is None else jnp.maximum(top[u], part)
        if n == spans - 1:
            top[u] = jnp.max(top[u], axis=0, keepdims=True) * factor

    def soften(u, n):
        dp = dot(v_rows[span_of(n), :], do_rows[cols_of(u), :], last)
        dp_ref[span_of(n), cols_of(u)] = dp
        for i, at, count in slots_of(u, n):
            e = jnp.exp2(s_ref[at, cols_of(u)] * factor - jnp.where(count > 0, top[u], 1e30))
            s_ref[at, cols_of(u)] = e
            weight = count.astype(jnp.float32)
            total = weight * fold(e, jnp.sum)
            delta = weight * fold(e * dp[i * BLOCK : (i + 1) * BLOCK], jnp.sum)
            sums[u] = (total, delta) if sums[u] is None else (sums[u][0] + total, sums[u][1] + delta)
        if n == spans - 1:
            inverse[u] = 1.0 / jnp.sum(sums[u][0], axis=0, keepdims=True)
            sums[u] = jnp.sum(sums[u][1], axis=0, keepdims=True) * inverse[u]

    def grads(u, n):
        probs, scores = [], []
        for _, at, count in slots_of(u, n):
            p = s_ref[at, cols_of(u)] * (count.astype(jnp.float32) * inverse[u])
            probs.append(p.astype(jnp.bfloat16))
            scores.append((p * (dp_ref[at, cols_of(u)] - sums[u])).astype(jnp.bfloat16))
        probs = jnp.concatenate(probs, axis=0)
        scores = jnp.concatenate(scores, axis=0)
        dv = dot(probs, do_rows[cols_of(u), :], plain)
        dk = dot(scores, q_rows[cols_of(u), :], plain)
        if u > 0:
            dv = dv + dv_ref[span_of(n), :]
            dk = dk + dk_ref[span_of(n), :]
        if u < units - 1:
            dv_ref[span_of(n), :] = dv
            dk_ref[span_of(n), :] = dk
        else:
            dk = dk * scale
            for place in range(span // PAIR):
                out = outs[n * (span // PAIR) + place]
                at = slice(place * PAIR, (place + 1) * PAIR)
                out[:, 0:HEAD_DIM] = dk[at].astype(out.dtype)
                out[:, HEAD_DIM : 2 * HEAD_DIM] = dv[at].astype(out.dtype)
        term = dot(k_rows[span_of(n), :], scores, first)
        dq[u] = term if dq[u] is None else dq[u] + term
        if n == spans - 1:
            out = (dq[u] * scale).T.astype(jnp.bfloat16)
            for i in range(unit // BLOCK):
                b, g = divmod(u * unit // BLOCK + i, GROUP)
                dq_outs[b][:, g * HEAD_DIM : (g + 1) * HEAD_DIM] = out[i * BLOCK : (i + 1) * BLOCK]

    stages = (score, soften, grads)
    for t in range(units + len(stages) - 1):
        for n in range(spans):
            for k, stage in enumerate(stages):
                if 0 <= t - k < units:
                    stage(t - k, n)


def attend(chunk, where, rand, queries, d_out, queries_other, dout_other, sources):
    heads = CHUNKS[chunk]
    qw = GROUP * HEAD_DIM
    kw = 2 * HEAD_DIM
    first = sum(CHUNKS[:chunk])
    q_spec = pl.BlockSpec((BLOCK, qw), lambda j, w, r: (0, w[0] * HEAD_HALF + first + j))
    kv_spec = pl.BlockSpec((PAIR, kw), lambda j, w, r: (0, j))
    dq_spec = pl.BlockSpec((BLOCK, qw), lambda j, w, r: (0, j))
    rows = GROUP * BLOCK
    pairs = 2 * heads * rows * PART * BLOCK
    dq_shape = jax.ShapeDtypeStruct((BLOCK, heads * qw), jnp.bfloat16)
    wide = jax.ShapeDtypeStruct((PAIR, heads * kw), jnp.float32)
    narrow = jax.ShapeDtypeStruct((PAIR, heads * kw), jnp.bfloat16)
    near_shape = narrow if DIRECT[chunk] else wide
    return pl.pallas_call(
        attend_kernel,
        out_shape=[dq_shape, dq_shape, wide, near_shape, narrow, narrow],
        grid_spec=pltpu.PrefetchScalarGridSpec(
            num_scalar_prefetch=2,
            grid=(heads,),
            in_specs=[q_spec] * 4 + [kv_spec] * 4,
            out_specs=[dq_spec] * 2 + [kv_spec] * 4,
            scratch_shapes=[
                pltpu.VMEM((PART * BLOCK, 2 * rows), jnp.float32),
                pltpu.VMEM((PART * BLOCK, 2 * rows), jnp.float32),
                pltpu.VMEM((2 * rows, HEAD_DIM), jnp.bfloat16),
                pltpu.VMEM((2 * rows, HEAD_DIM), jnp.bfloat16),
                pltpu.VMEM((PART * BLOCK, HEAD_DIM), jnp.bfloat16),
                pltpu.VMEM((PART * BLOCK, HEAD_DIM), jnp.bfloat16),
                pltpu.VMEM((PART * BLOCK, HEAD_DIM), jnp.float32),
                pltpu.VMEM((PART * BLOCK, HEAD_DIM), jnp.float32),
            ],
        ),
        name="attend",
        compiler_params=pltpu.CompilerParams(vmem_limit_bytes=VMEM_MIB * 2**20),
        cost_estimate=pl.CostEstimate(
            flops=10 * pairs * HEAD_DIM * 2, bytes_accessed=4 * 2**20, transcendentals=pairs
        ),
    )(where, rand, queries, d_out, queries_other, dout_other, *sources)


def finish_kernel(where_ref, *refs):
    chunks = len(CHUNKS)
    own, other, dq_own, dq_got = (refs[i * chunks : (i + 1) * chunks] for i in range(4))
    dq_ref, dk_ref, dv_ref = refs[4 * chunks :]
    half = where_ref[0]
    for value in range(2):

        @pl.when(half == value)
        def _():
            for piece, place in ((own, value), (other, 1 - value)):
                for chunk, heads in enumerate(CHUNKS):
                    for head in range(heads):
                        at = place * HALF_KV + (sum(CHUNKS[:chunk]) + head) * HEAD_DIM
                        from_col = 2 * head * HEAD_DIM
                        dk_ref[:, at : at + HEAD_DIM] = piece[chunk][
                            0:BLOCK, from_col : from_col + HEAD_DIM
                        ]
                        dv_ref[:, at : at + HEAD_DIM] = piece[chunk][
                            0:BLOCK, from_col + HEAD_DIM : from_col + 2 * HEAD_DIM
                        ]
            for piece, place in ((dq_own, value), (dq_got, 1 - value)):
                for chunk, heads in enumerate(CHUNKS):
                    at = place * HALF_Q + sum(CHUNKS[:chunk]) * GROUP * HEAD_DIM
                    width = heads * GROUP * HEAD_DIM
                    dq_ref[:, at : at + width] = piece[chunk][...]


def finish(where, own, other, dq_own, dq_got):
    return pl.pallas_call(
        finish_kernel,
        out_shape=[
            jax.ShapeDtypeStruct((BLOCK, 2 * HALF_Q), jnp.bfloat16),
            jax.ShapeDtypeStruct((BLOCK, 2 * HALF_KV), jnp.bfloat16),
            jax.ShapeDtypeStruct((BLOCK, 2 * HALF_KV), jnp.bfloat16),
        ],
        in_specs=[pl.BlockSpec(memory_space=pltpu.SMEM)]
        + [pl.BlockSpec(memory_space=pltpu.VMEM)] * (4 * len(CHUNKS)),
        out_specs=[pl.BlockSpec(memory_space=pltpu.VMEM)] * 3,
        name="finish",
        cost_estimate=pl.CostEstimate(flops=0, bytes_accessed=3 * 2**20, transcendentals=0),
    )(where, *own, *other, *dq_own, *dq_got)


def per_device_dense(queries, keys, values, d_out, rand_blocks):
    me = lax.axis_index("ctx") * 2 + lax.axis_index("uly")
    half = lax.axis_index("ctx") % 2
    where = jnp.stack([half, me]).astype(jnp.int32)
    rand = rand_blocks.reshape(PART * RANDOMS)
    keys_other = send(keys, SWAP_PERM)
    values_other = send(values, SWAP_PERM)
    pairs = pack_pairs(where, keys, values, keys_other, values_other)
    queries, d_out, pairs = lax.optimization_barrier((queries, d_out, pairs))
    queries_other = send(queries, SWAP_PERM)
    dout_other = send(d_out, SWAP_PERM)
    nears = [send(pair, NEAR_PERM) for pair in pairs]
    fars = [send(pair, FAR_PERM) for pair in pairs]
    corners = [send(near, FAR_PERM) for near in nears]
    own, other, dq_own, dq_got = [], [], [], []
    for chunk in range(len(CHUNKS)):
        dq_mine, dq_other, own_grads, near_grads, far_grads, corner_grads = attend(
            chunk,
            where,
            rand,
            queries,
            d_out,
            queries_other,
            dout_other,
            (pairs[chunk], nears[chunk], fars[chunk], corners[chunk]),
        )
        if DIRECT[chunk]:
            arrived = [send(corner_grads, CORNER_PERM), send(near_grads, NEAR_PERM)]
        else:
            from_corner = send(corner_grads, FAR_PERM)
            relayed = (near_grads + from_corner.astype(jnp.float32)).astype(jnp.bfloat16)
            arrived = [send(relayed, NEAR_PERM)]
        arrived.append(send(far_grads, FAR_PERM))
        total = own_grads + sum(x.astype(jnp.float32) for x in arrived)
        total = total.astype(jnp.bfloat16)
        own.append(total[:BLOCK])
        other.append(send(total[BLOCK:], SWAP_PERM))
        dq_own.append(dq_mine)
        dq_got.append(send(dq_other, SWAP_PERM))
    return tuple(finish(where, own, other, dq_own, dq_got))


def per_device(queries, keys, values, d_out, rand_blocks):
    dense = (
        lax.axis_size("ctx") == 4
        and lax.axis_size("uly") == 2
        and rand_blocks.shape[0] == PART
        and keys.shape == (BLOCK, 2 * HALF_KV)
    )
    plan = per_device_dense if dense else per_device_sparse
    return plan(queries, keys, values, d_out, rand_blocks)


def solution(mesh):
    in_specs = (
        P(("dp", "ctx", "uly"), None),
        P(("dp", "ctx", "uly"), None),
        P(("dp", "ctx", "uly"), None),
        P(("dp", "ctx", "uly"), None),
        P("dp", None),
    )
    out_specs = (
        P(("dp", "ctx", "uly"), None),
        P(("dp", "ctx", "uly"), None),
        P(("dp", "ctx", "uly"), None),
    )
    return jax.shard_map(
        per_device, mesh=mesh, in_specs=in_specs, out_specs=out_specs, check_vma=False
    )
```

```python
from functools import partial

import jax
import jax.numpy as jnp
from jax import lax
from jax.experimental import pallas as pl
from jax.experimental.pallas import tpu as pltpu
from jax.sharding import PartitionSpec as P

HEAD_DIM = 128
BLOCK = 128
WINDOW = 3
GLOBALS = 2
RANDOMS = 3
ENTRIES = 8
GROUP = 4


def listed_blocks(rand_blocks):
    total = rand_blocks.shape[0]
    block_ids = jnp.arange(total, dtype=jnp.int32)
    window_part = (
        block_ids[:, None] + jnp.arange(WINDOW, dtype=jnp.int32)[None, :] - WINDOW // 2
    ) % total
    global_part = jnp.broadcast_to(jnp.arange(GLOBALS, dtype=jnp.int32)[None, :], (total, GLOBALS))
    return jnp.concatenate([window_part, global_part, rand_blocks], axis=1)


def block_backward(sources, softmax_scale, inputs):
    query_blk, dout_blk, source_rows = inputs
    picked = jnp.take(sources, source_rows, axis=0)
    kv_width = picked.shape[-1] // 2
    kv_count = kv_width // HEAD_DIM
    key_sel = picked[..., :kv_width].reshape(ENTRIES, BLOCK, kv_count, HEAD_DIM)
    value_sel = picked[..., kv_width:].reshape(ENTRIES, BLOCK, kv_count, HEAD_DIM)
    query_four = query_blk.reshape(BLOCK, kv_count, GROUP, HEAD_DIM)
    dout_four = dout_blk.reshape(BLOCK, kv_count, GROUP, HEAD_DIM)
    scores = jnp.einsum("tkgd,eskd->kgtes", query_four, key_sel, preferred_element_type=jnp.float32)
    scores = scores.reshape(kv_count, GROUP, BLOCK, ENTRIES * BLOCK) * softmax_scale
    row_max = jnp.max(scores, axis=-1, keepdims=True)
    exp_scores = jnp.exp(scores - row_max)
    prob_rows = exp_scores / jnp.sum(exp_scores, axis=-1, keepdims=True)
    grad_probs = jnp.einsum(
        "tkgd,eskd->kgtes", dout_four, value_sel, preferred_element_type=jnp.float32
    )
    grad_probs = grad_probs.reshape(kv_count, GROUP, BLOCK, ENTRIES * BLOCK)
    row_delta = jnp.sum(prob_rows * grad_probs, axis=-1, keepdims=True)
    grad_scores = (
        (prob_rows * (grad_probs - row_delta))
        .astype(jnp.bfloat16)
        .reshape(kv_count, GROUP, BLOCK, ENTRIES, BLOCK)
    )
    probs_low = prob_rows.astype(jnp.bfloat16).reshape(kv_count, GROUP, BLOCK, ENTRIES, BLOCK)
    grad_values = jnp.einsum(
        "kgtes,tkgd->eskd", probs_low, dout_four, preferred_element_type=jnp.float32
    )
    grad_keys = (
        jnp.einsum("kgtes,tkgd->eskd", grad_scores, query_four, preferred_element_type=jnp.float32)
        * softmax_scale
    )
    grad_query = (
        jnp.einsum("kgtes,eskd->tkgd", grad_scores, key_sel, preferred_element_type=jnp.float32)
        * softmax_scale
    )
    partials = jnp.concatenate(
        [
            grad_keys.reshape(ENTRIES, BLOCK, kv_width),
            grad_values.reshape(ENTRIES, BLOCK, kv_width),
        ],
        axis=-1,
    )
    return (partials, grad_query.reshape(BLOCK, kv_count * GROUP * HEAD_DIM))


def per_device_sparse(queries, keys, values, d_out, rand_blocks):
    softmax_scale = HEAD_DIM ** (-0.5)
    groups = lax.axis_size("ctx")
    my_group = lax.axis_index("ctx")
    queries_here, dout_here, keys_here, values_here = (
        lax.all_to_all(queries, "uly", split_axis=1, concat_axis=0, tiled=True),
        lax.all_to_all(d_out, "uly", split_axis=1, concat_axis=0, tiled=True),
        lax.all_to_all(keys, "uly", split_axis=1, concat_axis=0, tiled=True),
        lax.all_to_all(values, "uly", split_axis=1, concat_axis=0, tiled=True),
    )
    tokens_here = keys_here.shape[0]
    per_group = tokens_here // BLOCK
    kv_width = keys_here.shape[1]
    local_blocks = jnp.concatenate([keys_here, values_here], axis=1).reshape(
        per_group, BLOCK, 2 * kv_width
    )
    listed = listed_blocks(rand_blocks)
    owners = listed // per_group
    offsets = listed % per_group
    requester = (jnp.arange(listed.shape[0], dtype=jnp.int32) // per_group)[:, None]
    entry_ids = jnp.arange(ENTRIES, dtype=jnp.int32)
    is_global = (entry_ids >= WINDOW) & (entry_ids < WINDOW + GLOBALS)
    entry_global = jnp.tile(is_global, per_group)
    global_slot = jnp.tile(entry_ids - WINDOW, per_group)
    rand_capacity = per_group * RANDOMS // groups + 1
    remote = owners != requester
    capacity = rand_capacity + GLOBALS
    lead_slots = GLOBALS
    owners = owners.reshape(groups, per_group * ENTRIES)
    offsets = offsets.reshape(groups, per_group * ENTRIES)
    remote = remote.reshape(groups, per_group * ENTRIES)
    counted = remote & jnp.logical_not(entry_global)[None, :]
    owner_hot = (
        (owners[:, :, None] == jnp.arange(groups, dtype=jnp.int32)[None, None, :])
        & counted[:, :, None]
    ).astype(jnp.int32)
    rand_slot = jnp.sum((jnp.cumsum(owner_hot, axis=1) - 1) * owner_hot, axis=2) + lead_slots
    slot_index = jnp.where(entry_global[None, :], global_slot[None, :], rand_slot)
    for_me = remote & (owners == my_group)
    slot_match = (
        slot_index[:, :, None, None] == jnp.arange(capacity, dtype=jnp.int32)[None, None, :, None]
    )
    block_match = (
        offsets[:, :, None, None] == jnp.arange(per_group, dtype=jnp.int32)[None, None, None, :]
    )
    slot_picker = jnp.minimum(
        jnp.sum((for_me[:, :, None, None] & slot_match & block_match).astype(jnp.int32), axis=1), 1
    )
    outgoing = jnp.einsum(
        "csb,bxd->csxd",
        slot_picker.astype(jnp.bfloat16),
        local_blocks,
        preferred_element_type=jnp.float32,
    ).astype(jnp.bfloat16)
    incoming = lax.all_to_all(outgoing, "ctx", split_axis=0, concat_axis=0, tiled=True)
    my_owner = lax.dynamic_index_in_dim(owners, my_group, 0, keepdims=False)
    my_slot = lax.dynamic_index_in_dim(slot_index, my_group, 0, keepdims=False)
    my_offset = lax.dynamic_index_in_dim(offsets, my_group, 0, keepdims=False)
    my_remote = lax.dynamic_index_in_dim(remote, my_group, 0, keepdims=False)
    source_rows = jnp.where(my_remote, per_group + my_owner * capacity + my_slot, my_offset)
    pieces = [local_blocks, incoming.reshape(groups * capacity, BLOCK, 2 * kv_width)]
    sources = jnp.concatenate(pieces, axis=0)
    source_count = sources.shape[0]
    query_blocks = queries_here.reshape(per_group, BLOCK, queries_here.shape[1])
    dout_blocks = dout_here.reshape(per_group, BLOCK, dout_here.shape[1])
    partials, grad_query = lax.map(
        partial(block_backward, sources, softmax_scale),
        (query_blocks, dout_blocks, source_rows.reshape(per_group, ENTRIES)),
    )
    source_hot = (
        source_rows[:, None] == jnp.arange(source_count, dtype=jnp.int32)[None, :]
    ).astype(jnp.float32)
    source_grads = jnp.einsum(
        "ms,mxd->sxd",
        source_hot,
        partials.reshape(per_group * ENTRIES, BLOCK, 2 * kv_width),
        precision=lax.Precision.HIGHEST,
    )
    own_grads = source_grads[:per_group]
    sent_grads = source_grads[per_group : per_group + groups * capacity].reshape(
        groups, capacity, BLOCK, 2 * kv_width
    )
    returned = lax.all_to_all(sent_grads, "ctx", split_axis=0, concat_axis=0, tiled=True)
    own_grads = own_grads + jnp.einsum(
        "csb,csxd->bxd", slot_picker.astype(jnp.float32), returned, precision=lax.Precision.HIGHEST
    )
    query_grads = grad_query.reshape(tokens_here, queries_here.shape[1]).astype(jnp.bfloat16)
    key_grads = own_grads[..., :kv_width].reshape(tokens_here, kv_width).astype(jnp.bfloat16)
    value_grads = own_grads[..., kv_width:].reshape(tokens_here, kv_width).astype(jnp.bfloat16)
    d_queries, d_keys, d_values = (
        lax.all_to_all(query_grads, "uly", split_axis=0, concat_axis=1, tiled=True),
        lax.all_to_all(key_grads, "uly", split_axis=0, concat_axis=1, tiled=True),
        lax.all_to_all(value_grads, "uly", split_axis=0, concat_axis=1, tiled=True),
    )
    return (d_queries, d_keys, d_values)


LOG2E = 1.4426950408889634
PART = 8
HEAD_HALF = 4
CHUNKS = (2, 2)
VMEM_MIB = 48
PIN2 = PIN3 = lambda x: x
OUT = lambda x: x
PIN = partial(pltpu.with_memory_space_constraint, memory_space=pltpu.HBM)
HALF_Q = HEAD_HALF * GROUP * HEAD_DIM
HALF_KV = HEAD_HALF * HEAD_DIM
PAIR = 2 * BLOCK
AXES = ("ctx", "uly")

SWAP = 2


def perm_to(first, second):
    return [(i, i ^ (second if i & SWAP else first)) for i in range(PART)]


SWAP_PERM = perm_to(SWAP, SWAP)
CORNER_PERM = perm_to(5, 5)
NEAR_PERM = perm_to(4, 1)
FAR_PERM = perm_to(1, 4)


def send(array, perm):
    return lax.ppermute(array, AXES, perm)


def move_all(copies):
    for copy in copies:
        copy.start()
    for copy in copies:
        copy.wait()


def lanes(start, width):
    return pl.ds(pl.multiple_of(start, HEAD_DIM), width)


def pack_kernel(where_ref, k_ref, v_ref, ko_ref, vo_ref, *refs):
    outs, sems = refs[:-1], refs[-1]
    copies = []
    for chunk, heads in enumerate(CHUNKS):
        for head in range(heads):
            at = where_ref[0] * HALF_KV + (sum(CHUNKS[:chunk]) + head) * HEAD_DIM
            for row, pieces in enumerate(((k_ref, v_ref), (ko_ref, vo_ref))):
                for side, ref in enumerate(pieces):
                    to = outs[chunk].at[
                        row * BLOCK : (row + 1) * BLOCK,
                        (2 * head + side) * HEAD_DIM : (2 * head + side + 1) * HEAD_DIM,
                    ]
                    sem = sems.at[len(copies)]
                    source = ref.at[:, lanes(at, HEAD_DIM)]
                    copies.append(pltpu.make_async_copy(source, to, sem))
    move_all(copies)


def pack_pairs(where, keys, values, keys_other, values_other):
    return pl.pallas_call(
        pack_kernel,
        out_shape=[
            jax.ShapeDtypeStruct((PAIR, 2 * HEAD_DIM * heads), jnp.bfloat16) for heads in CHUNKS
        ],
        in_specs=[pl.BlockSpec(memory_space=pltpu.SMEM)] + [pl.BlockSpec(memory_space=pl.ANY)] * 4,
        out_specs=[pl.BlockSpec(memory_space=pltpu.VMEM)] * len(CHUNKS),
        scratch_shapes=[pltpu.SemaphoreType.DMA((4 * HEAD_HALF,))],
        name="pack_pairs",
        compiler_params=pltpu.CompilerParams(vmem_limit_bytes=VMEM_MIB * 2**20),
        cost_estimate=pl.CostEstimate(flops=0, bytes_accessed=2**20, transcendentals=0),
    )(where, PIN(keys), PIN(values), keys_other, values_other)


def attend_kernel(
    where_ref,
    rand_ref,
    q_ref,
    do_ref,
    qo_ref,
    doo_ref,
    pair_ref,
    near_ref,
    far_ref,
    corner_ref,
    dq_ref,
    dqo_ref,
    own_out,
    near_out,
    far_out,
    corner_out,
    s_ref,
    dp_ref,
    q_rows,
    do_rows,
    k_rows,
    v_rows,
    dk_ref,
    dv_ref,
):
    scale = HEAD_DIM ** (-0.5)
    factor = scale * LOG2E
    half = where_ref[0]
    me = where_ref[1]
    near = 4 - 3 * half
    far = 1 + 3 * half
    deltas = (0, near, far, near ^ far)
    outs = (own_out, near_out, far_out, corner_out)
    dq_outs = (dq_ref, dqo_ref)
    rows = GROUP * BLOCK
    unit = rows // 2
    units = 2 * rows // unit
    span = 4 * BLOCK
    spans = PART * BLOCK // span
    last = (((1,), (1,)), ((), ()))
    plain = (((1,), (0,)), ((), ()))
    first = (((0,), (0,)), ((), ()))
    dot = partial(lax.dot_general, preferred_element_type=jnp.float32)

    for b, (q, do) in enumerate(((q_ref, do_ref), (qo_ref, doo_ref))):
        for g in range(GROUP):
            at = slice(b * rows + g * BLOCK, b * rows + (g + 1) * BLOCK)
            q_rows[at, :] = q[:, g * HEAD_DIM : (g + 1) * HEAD_DIM]
            do_rows[at, :] = do[:, g * HEAD_DIM : (g + 1) * HEAD_DIM]
    for place, source in enumerate((pair_ref, near_ref, far_ref, corner_ref)):
        at = slice(place * PAIR, (place + 1) * PAIR)
        k_rows[at, :] = source[:, 0:HEAD_DIM]
        v_rows[at, :] = source[:, HEAD_DIM : 2 * HEAD_DIM]

    def count_of(b, slot):
        block = me ^ (SWAP * b)
        listed = me ^ deltas[slot // 2] ^ (SWAP * (slot % 2))
        total = (listed < GLOBALS).astype(jnp.int32)
        for w in range(WINDOW):
            total += (lax.rem(block + (w - WINDOW // 2 + PART), PART) == listed).astype(jnp.int32)
        for r in range(RANDOMS):
            total += (rand_ref[block * RANDOMS + r] == listed).astype(jnp.int32)
        return total

    counts = [[count_of(b, slot) for slot in range(PART)] for b in range(2)]

    def slots_of(u, n):
        for i in range(span // BLOCK):
            slot = n * (span // BLOCK) + i
            yield i, slice(slot * BLOCK, (slot + 1) * BLOCK), counts[u * unit // rows][slot]

    def fold(x, op):
        return op(x.reshape(BLOCK // 8, 8, unit), axis=0)

    def cols_of(u):
        return slice(u * unit, (u + 1) * unit)

    def span_of(n):
        return slice(n * span, (n + 1) * span)

    top, sums, inverse, dq = [None] * units, [None] * units, [None] * units, [None] * units

    def score(u, n):
        s = dot(k_rows[span_of(n), :], q_rows[cols_of(u), :], last)
        s_ref[span_of(n), cols_of(u)] = s
        for i, _, count in slots_of(u, n):
            part = fold(s[i * BLOCK : (i + 1) * BLOCK], jnp.max)
            part = jnp.where(count > 0, part, -1e30)
            top[u] = part if top[u] is None else jnp.maximum(top[u], part)
        if n == spans - 1:
            top[u] = jnp.max(top[u], axis=0, keepdims=True) * factor

    def soften(u, n):
        dp = dot(v_rows[span_of(n), :], do_rows[cols_of(u), :], last)
        dp_ref[span_of(n), cols_of(u)] = dp
        for i, at, count in slots_of(u, n):
            e = jnp.exp2(s_ref[at, cols_of(u)] * factor - jnp.where(count > 0, top[u], 1e30))
            s_ref[at, cols_of(u)] = e
            weight = count.astype(jnp.float32)
            total = weight * fold(e, jnp.sum)
            delta = weight * fold(e * dp[i * BLOCK : (i + 1) * BLOCK], jnp.sum)
            sums[u] = (total, delta) if sums[u] is None else (sums[u][0] + total, sums[u][1] + delta)
        if n == spans - 1:
            inverse[u] = 1.0 / jnp.sum(sums[u][0], axis=0, keepdims=True)
            sums[u] = jnp.sum(sums[u][1], axis=0, keepdims=True) * inverse[u]

    def grads(u, n):
        probs, scores = [], []
        for _, at, count in slots_of(u, n):
            p = s_ref[at, cols_of(u)] * (count.astype(jnp.float32) * inverse[u])
            probs.append(p.astype(jnp.bfloat16))
            scores.append((p * (dp_ref[at, cols_of(u)] - sums[u])).astype(jnp.bfloat16))
        probs = jnp.concatenate(probs, axis=0)
        scores = jnp.concatenate(scores, axis=0)
        dv = dot(probs, do_rows[cols_of(u), :], plain)
        dk = dot(scores, q_rows[cols_of(u), :], plain)
        if u > 0:
            dv = dv + dv_ref[span_of(n), :]
            dk = dk + dk_ref[span_of(n), :]
        if u < units - 1:
            dv_ref[span_of(n), :] = dv
            dk_ref[span_of(n), :] = dk
        else:
            dk = dk * scale
            for place in range(span // PAIR):
                out = outs[n * (span // PAIR) + place]
                at = slice(place * PAIR, (place + 1) * PAIR)
                out[:, 0:HEAD_DIM] = dk[at].astype(out.dtype)
                out[:, HEAD_DIM : 2 * HEAD_DIM] = dv[at].astype(out.dtype)
        term = dot(k_rows[span_of(n), :], scores, first)
        dq[u] = term if dq[u] is None else dq[u] + term
        if n == spans - 1:
            out = (dq[u] * scale).T.astype(jnp.bfloat16)
            for i in range(unit // BLOCK):
                b, g = divmod(u * unit // BLOCK + i, GROUP)
                dq_outs[b][:, g * HEAD_DIM : (g + 1) * HEAD_DIM] = out[i * BLOCK : (i + 1) * BLOCK]

    stages = (score, soften, grads)
    for t in range(units + len(stages) - 1):
        for n in range(spans):
            for k, stage in enumerate(stages):
                if 0 <= t - k < units:
                    stage(t - k, n)


def attend(chunk, where, rand, queries, d_out, queries_other, dout_other, sources):
    heads = CHUNKS[chunk]
    qw = GROUP * HEAD_DIM
    kw = 2 * HEAD_DIM
    first = sum(CHUNKS[:chunk])
    q_spec = pl.BlockSpec((BLOCK, qw), lambda j, w, r: (0, w[0] * HEAD_HALF + first + j))
    kv_spec = pl.BlockSpec((PAIR, kw), lambda j, w, r: (0, j))
    dq_spec = pl.BlockSpec((BLOCK, qw), lambda j, w, r: (0, j))
    rows = GROUP * BLOCK
    pairs = 2 * heads * rows * PART * BLOCK
    dq_shape = jax.ShapeDtypeStruct((BLOCK, heads * qw), jnp.bfloat16)
    wide = jax.ShapeDtypeStruct((PAIR, heads * kw), jnp.float32)
    narrow = jax.ShapeDtypeStruct((PAIR, heads * kw), jnp.bfloat16)
    return pl.pallas_call(
        attend_kernel,
        out_shape=[OUT(dq_shape), OUT(dq_shape), wide, narrow, narrow, narrow],
        grid_spec=pltpu.PrefetchScalarGridSpec(
            num_scalar_prefetch=2,
            grid=(heads,),
            in_specs=[q_spec] * 4 + [kv_spec] * 4,
            out_specs=[dq_spec] * 2 + [kv_spec] * 4,
            scratch_shapes=[
                pltpu.VMEM((PART * BLOCK, 2 * rows), jnp.float32),
                pltpu.VMEM((PART * BLOCK, 2 * rows), jnp.float32),
                pltpu.VMEM((2 * rows, HEAD_DIM), jnp.bfloat16),
                pltpu.VMEM((2 * rows, HEAD_DIM), jnp.bfloat16),
                pltpu.VMEM((PART * BLOCK, HEAD_DIM), jnp.bfloat16),
                pltpu.VMEM((PART * BLOCK, HEAD_DIM), jnp.bfloat16),
                pltpu.VMEM((PART * BLOCK, HEAD_DIM), jnp.float32),
                pltpu.VMEM((PART * BLOCK, HEAD_DIM), jnp.float32),
            ],
        ),
        name="attend",
        compiler_params=pltpu.CompilerParams(vmem_limit_bytes=VMEM_MIB * 2**20),
        cost_estimate=pl.CostEstimate(
            flops=10 * pairs * HEAD_DIM * 2, bytes_accessed=4 * 2**20, transcendentals=pairs
        ),
    )(where, rand, *map(PIN, (queries, d_out, queries_other, dout_other)), *map(PIN2, sources))


def place_kernel(columns, where_ref, *refs):
    inputs = refs[: len(columns) * 2]
    outs, sems = refs[len(columns) * 2 : -1], refs[-1]
    copies = []
    for i, pieces in enumerate(columns):
        for half in range(2):
            place = where_ref[0] ^ half
            for out, at, start, width in pieces:
                at = at + place * (outs[out].shape[1] // 2)
                source = inputs[2 * i + half].at[:, start : start + width]
                to = outs[out].at[:, lanes(at, width)]
                copies.append(pltpu.make_async_copy(source, to, sems.at[len(copies)]))
    move_all(copies)


def place(columns, where, inputs, widths, name):
    count = 2 * sum(len(pieces) for pieces in columns)
    return pl.pallas_call(
        partial(place_kernel, columns),
        out_shape=[jax.ShapeDtypeStruct((BLOCK, width), jnp.bfloat16) for width in widths],
        in_specs=[pl.BlockSpec(memory_space=pltpu.SMEM)]
        + [pl.BlockSpec(memory_space=pl.ANY)] * len(inputs),
        out_specs=[pl.BlockSpec(memory_space=pltpu.VMEM)] * len(widths),
        scratch_shapes=[pltpu.SemaphoreType.DMA((count,))],
        name=name,
        cost_estimate=pl.CostEstimate(flops=0, bytes_accessed=2**20, transcendentals=0),
    )(where, *inputs)


def place_queries(where, own, got):
    columns, inputs = [], []
    for chunk, heads in enumerate(CHUNKS):
        width = heads * GROUP * HEAD_DIM
        columns.append([(0, sum(CHUNKS[:chunk]) * GROUP * HEAD_DIM, 0, width)])
        inputs += [own[chunk], got[chunk]]
    return place(columns, where, inputs, [2 * HALF_Q], "place_queries")[0]


def place_pairs(where, own, got):
    columns, inputs = [], []
    for chunk, heads in enumerate(CHUNKS):
        pieces = []
        for head in range(heads):
            at = (sum(CHUNKS[:chunk]) + head) * HEAD_DIM
            for side in range(2):
                pieces.append((side, at, (2 * head + side) * HEAD_DIM, HEAD_DIM))
        columns.append(pieces)
        inputs += [own[chunk], got[chunk]]
    return place(columns, where, inputs, [2 * HALF_KV] * 2, "place_pairs")


def per_device_dense(queries, keys, values, d_out, rand_blocks):
    me = lax.axis_index("ctx") * 2 + lax.axis_index("uly")
    half = lax.axis_index("ctx") % 2
    where = jnp.stack([half, me]).astype(jnp.int32)
    rand = rand_blocks.reshape(PART * RANDOMS)
    keys_other = send(keys, SWAP_PERM)
    values_other = send(values, SWAP_PERM)
    pairs = pack_pairs(where, keys, values, keys_other, values_other)
    queries, d_out, pairs = lax.optimization_barrier((queries, d_out, pairs))
    queries_other = send(queries, SWAP_PERM)
    dout_other = send(d_out, SWAP_PERM)
    nears = [send(pair, NEAR_PERM) for pair in pairs]
    fars = [send(pair, FAR_PERM) for pair in pairs]
    corners = [send(near, FAR_PERM) for near in nears]
    terms, dq_own, dq_got = [], [], []
    for chunk in range(len(CHUNKS)):
        dq_mine, dq_other, own_grads, near_grads, far_grads, corner_grads = attend(
            chunk,
            where,
            rand,
            queries,
            d_out,
            queries_other,
            dout_other,
            (pairs[chunk], nears[chunk], fars[chunk], corners[chunk]),
        )
        arrived = [
            send(corner_grads, CORNER_PERM),
            send(near_grads, NEAR_PERM),
            send(far_grads, FAR_PERM),
        ]
        terms.append((own_grads, arrived))
        dq_own.append(dq_mine)
        dq_got.append(send(dq_other, SWAP_PERM))
    d_queries = place_queries(where, dq_own, dq_got)
    terms[-1], d_queries = lax.optimization_barrier((terms[-1], d_queries))
    own, other = [], []
    for own_grads, arrived in terms:
        mine, theirs = (
            sum((x[at].astype(jnp.float32) for x in arrived), own_grads[at]).astype(jnp.bfloat16)
            for at in (slice(0, BLOCK), slice(BLOCK, PAIR))
        )
        own.append(mine)
        other.append(send(theirs, SWAP_PERM))
    d_keys, d_values = place_pairs(where, own, other)
    return (d_queries, d_keys, d_values)


def per_device(queries, keys, values, d_out, rand_blocks):
    dense = (
        lax.axis_size("ctx") == 4
        and lax.axis_size("uly") == 2
        and rand_blocks.shape[0] == PART
        and keys.shape == (BLOCK, 2 * HALF_KV)
    )
    plan = per_device_dense if dense else per_device_sparse
    return plan(queries, keys, values, d_out, rand_blocks)


def solution(mesh):
    in_specs = (
        P(("dp", "ctx", "uly"), None),
        P(("dp", "ctx", "uly"), None),
        P(("dp", "ctx", "uly"), None),
        P(("dp", "ctx", "uly"), None),
        P("dp", None),
    )
    out_specs = (
        P(("dp", "ctx", "uly"), None),
        P(("dp", "ctx", "uly"), None),
        P(("dp", "ctx", "uly"), None),
    )
    return jax.shard_map(
        per_device, mesh=mesh, in_specs=in_specs, out_specs=out_specs, check_vma=False
    )
```

```python
from functools import partial

import jax
import jax.numpy as jnp
from jax import lax
from jax.experimental import pallas as pl
from jax.experimental.pallas import tpu as pltpu
from jax.sharding import PartitionSpec as P

HEAD_DIM = 128
BLOCK = 128
WINDOW = 3
GLOBALS = 2
RANDOMS = 3
ENTRIES = 8
GROUP = 4


def listed_blocks(rand_blocks):
    total = rand_blocks.shape[0]
    block_ids = jnp.arange(total, dtype=jnp.int32)
    window_part = (
        block_ids[:, None] + jnp.arange(WINDOW, dtype=jnp.int32)[None, :] - WINDOW // 2
    ) % total
    global_part = jnp.broadcast_to(jnp.arange(GLOBALS, dtype=jnp.int32)[None, :], (total, GLOBALS))
    return jnp.concatenate([window_part, global_part, rand_blocks], axis=1)


def block_backward(sources, softmax_scale, inputs):
    query_blk, dout_blk, source_rows = inputs
    picked = jnp.take(sources, source_rows, axis=0)
    kv_width = picked.shape[-1] // 2
    kv_count = kv_width // HEAD_DIM
    key_sel = picked[..., :kv_width].reshape(ENTRIES, BLOCK, kv_count, HEAD_DIM)
    value_sel = picked[..., kv_width:].reshape(ENTRIES, BLOCK, kv_count, HEAD_DIM)
    query_four = query_blk.reshape(BLOCK, kv_count, GROUP, HEAD_DIM)
    dout_four = dout_blk.reshape(BLOCK, kv_count, GROUP, HEAD_DIM)
    scores = jnp.einsum("tkgd,eskd->kgtes", query_four, key_sel, preferred_element_type=jnp.float32)
    scores = scores.reshape(kv_count, GROUP, BLOCK, ENTRIES * BLOCK) * softmax_scale
    row_max = jnp.max(scores, axis=-1, keepdims=True)
    exp_scores = jnp.exp(scores - row_max)
    prob_rows = exp_scores / jnp.sum(exp_scores, axis=-1, keepdims=True)
    grad_probs = jnp.einsum(
        "tkgd,eskd->kgtes", dout_four, value_sel, preferred_element_type=jnp.float32
    )
    grad_probs = grad_probs.reshape(kv_count, GROUP, BLOCK, ENTRIES * BLOCK)
    row_delta = jnp.sum(prob_rows * grad_probs, axis=-1, keepdims=True)
    grad_scores = (
        (prob_rows * (grad_probs - row_delta))
        .astype(jnp.bfloat16)
        .reshape(kv_count, GROUP, BLOCK, ENTRIES, BLOCK)
    )
    probs_low = prob_rows.astype(jnp.bfloat16).reshape(kv_count, GROUP, BLOCK, ENTRIES, BLOCK)
    grad_values = jnp.einsum(
        "kgtes,tkgd->eskd", probs_low, dout_four, preferred_element_type=jnp.float32
    )
    grad_keys = (
        jnp.einsum("kgtes,tkgd->eskd", grad_scores, query_four, preferred_element_type=jnp.float32)
        * softmax_scale
    )
    grad_query = (
        jnp.einsum("kgtes,eskd->tkgd", grad_scores, key_sel, preferred_element_type=jnp.float32)
        * softmax_scale
    )
    partials = jnp.concatenate(
        [
            grad_keys.reshape(ENTRIES, BLOCK, kv_width),
            grad_values.reshape(ENTRIES, BLOCK, kv_width),
        ],
        axis=-1,
    )
    return (partials, grad_query.reshape(BLOCK, kv_count * GROUP * HEAD_DIM))


def per_device_sparse(queries, keys, values, d_out, rand_blocks):
    softmax_scale = HEAD_DIM ** (-0.5)
    groups = lax.axis_size("ctx")
    my_group = lax.axis_index("ctx")
    queries_here, dout_here, keys_here, values_here = (
        lax.all_to_all(queries, "uly", split_axis=1, concat_axis=0, tiled=True),
        lax.all_to_all(d_out, "uly", split_axis=1, concat_axis=0, tiled=True),
        lax.all_to_all(keys, "uly", split_axis=1, concat_axis=0, tiled=True),
        lax.all_to_all(values, "uly", split_axis=1, concat_axis=0, tiled=True),
    )
    tokens_here = keys_here.shape[0]
    per_group = tokens_here // BLOCK
    kv_width = keys_here.shape[1]
    local_blocks = jnp.concatenate([keys_here, values_here], axis=1).reshape(
        per_group, BLOCK, 2 * kv_width
    )
    listed = listed_blocks(rand_blocks)
    owners = listed // per_group
    offsets = listed % per_group
    requester = (jnp.arange(listed.shape[0], dtype=jnp.int32) // per_group)[:, None]
    entry_ids = jnp.arange(ENTRIES, dtype=jnp.int32)
    is_global = (entry_ids >= WINDOW) & (entry_ids < WINDOW + GLOBALS)
    entry_global = jnp.tile(is_global, per_group)
    global_slot = jnp.tile(entry_ids - WINDOW, per_group)
    rand_capacity = per_group * RANDOMS // groups + 1
    remote = owners != requester
    capacity = rand_capacity + GLOBALS
    lead_slots = GLOBALS
    owners = owners.reshape(groups, per_group * ENTRIES)
    offsets = offsets.reshape(groups, per_group * ENTRIES)
    remote = remote.reshape(groups, per_group * ENTRIES)
    counted = remote & jnp.logical_not(entry_global)[None, :]
    owner_hot = (
        (owners[:, :, None] == jnp.arange(groups, dtype=jnp.int32)[None, None, :])
        & counted[:, :, None]
    ).astype(jnp.int32)
    rand_slot = jnp.sum((jnp.cumsum(owner_hot, axis=1) - 1) * owner_hot, axis=2) + lead_slots
    slot_index = jnp.where(entry_global[None, :], global_slot[None, :], rand_slot)
    for_me = remote & (owners == my_group)
    slot_match = (
        slot_index[:, :, None, None] == jnp.arange(capacity, dtype=jnp.int32)[None, None, :, None]
    )
    block_match = (
        offsets[:, :, None, None] == jnp.arange(per_group, dtype=jnp.int32)[None, None, None, :]
    )
    slot_picker = jnp.minimum(
        jnp.sum((for_me[:, :, None, None] & slot_match & block_match).astype(jnp.int32), axis=1), 1
    )
    outgoing = jnp.einsum(
        "csb,bxd->csxd",
        slot_picker.astype(jnp.bfloat16),
        local_blocks,
        preferred_element_type=jnp.float32,
    ).astype(jnp.bfloat16)
    incoming = lax.all_to_all(outgoing, "ctx", split_axis=0, concat_axis=0, tiled=True)
    my_owner = lax.dynamic_index_in_dim(owners, my_group, 0, keepdims=False)
    my_slot = lax.dynamic_index_in_dim(slot_index, my_group, 0, keepdims=False)
    my_offset = lax.dynamic_index_in_dim(offsets, my_group, 0, keepdims=False)
    my_remote = lax.dynamic_index_in_dim(remote, my_group, 0, keepdims=False)
    source_rows = jnp.where(my_remote, per_group + my_owner * capacity + my_slot, my_offset)
    pieces = [local_blocks, incoming.reshape(groups * capacity, BLOCK, 2 * kv_width)]
    sources = jnp.concatenate(pieces, axis=0)
    source_count = sources.shape[0]
    query_blocks = queries_here.reshape(per_group, BLOCK, queries_here.shape[1])
    dout_blocks = dout_here.reshape(per_group, BLOCK, dout_here.shape[1])
    partials, grad_query = lax.map(
        partial(block_backward, sources, softmax_scale),
        (query_blocks, dout_blocks, source_rows.reshape(per_group, ENTRIES)),
    )
    source_hot = (
        source_rows[:, None] == jnp.arange(source_count, dtype=jnp.int32)[None, :]
    ).astype(jnp.float32)
    source_grads = jnp.einsum(
        "ms,mxd->sxd",
        source_hot,
        partials.reshape(per_group * ENTRIES, BLOCK, 2 * kv_width),
        precision=lax.Precision.HIGHEST,
    )
    own_grads = source_grads[:per_group]
    sent_grads = source_grads[per_group : per_group + groups * capacity].reshape(
        groups, capacity, BLOCK, 2 * kv_width
    )
    returned = lax.all_to_all(sent_grads, "ctx", split_axis=0, concat_axis=0, tiled=True)
    own_grads = own_grads + jnp.einsum(
        "csb,csxd->bxd", slot_picker.astype(jnp.float32), returned, precision=lax.Precision.HIGHEST
    )
    query_grads = grad_query.reshape(tokens_here, queries_here.shape[1]).astype(jnp.bfloat16)
    key_grads = own_grads[..., :kv_width].reshape(tokens_here, kv_width).astype(jnp.bfloat16)
    value_grads = own_grads[..., kv_width:].reshape(tokens_here, kv_width).astype(jnp.bfloat16)
    d_queries, d_keys, d_values = (
        lax.all_to_all(query_grads, "uly", split_axis=0, concat_axis=1, tiled=True),
        lax.all_to_all(key_grads, "uly", split_axis=0, concat_axis=1, tiled=True),
        lax.all_to_all(value_grads, "uly", split_axis=0, concat_axis=1, tiled=True),
    )
    return (d_queries, d_keys, d_values)


LOG2E = 1.4426950408889634
PART = 8
HEAD_HALF = 4
CHUNKS = (2, 2)
VMEM_MIB = 48
PIN2 = PIN3 = lambda x: x
OUT = lambda x: x
PIN = partial(pltpu.with_memory_space_constraint, memory_space=pltpu.HBM)
HALF_Q = HEAD_HALF * GROUP * HEAD_DIM
HALF_KV = HEAD_HALF * HEAD_DIM
PAIR = 2 * BLOCK
AXES = ("ctx", "uly")

SWAP = 2


def perm_to(first, second):
    return [(i, i ^ (second if i & SWAP else first)) for i in range(PART)]


SWAP_PERM = perm_to(SWAP, SWAP)
CORNER_PERM = perm_to(5, 5)
NEAR_PERM = perm_to(4, 1)
FAR_PERM = perm_to(1, 4)


def send(array, perm):
    return lax.ppermute(array, AXES, perm)


def move_all(copies):
    for copy in copies:
        copy.start()
    for copy in copies:
        copy.wait()


def lanes(start, width):
    return pl.ds(pl.multiple_of(start, HEAD_DIM), width)


def pack_kernel(where_ref, k_ref, v_ref, ko_ref, vo_ref, *refs):
    outs, sems = refs[:-1], refs[-1]
    copies = []
    for chunk, heads in enumerate(CHUNKS):
        for head in range(heads):
            at = where_ref[0] * HALF_KV + (sum(CHUNKS[:chunk]) + head) * HEAD_DIM
            for row, pieces in enumerate(((k_ref, v_ref), (ko_ref, vo_ref))):
                for side, ref in enumerate(pieces):
                    to = outs[chunk].at[
                        row * BLOCK : (row + 1) * BLOCK,
                        (2 * head + side) * HEAD_DIM : (2 * head + side + 1) * HEAD_DIM,
                    ]
                    sem = sems.at[len(copies)]
                    source = ref.at[:, lanes(at, HEAD_DIM)]
                    copies.append(pltpu.make_async_copy(source, to, sem))
    move_all(copies)


def pack_pairs(where, keys, values, keys_other, values_other):
    return pl.pallas_call(
        pack_kernel,
        out_shape=[
            jax.ShapeDtypeStruct((PAIR, 2 * HEAD_DIM * heads), jnp.bfloat16) for heads in CHUNKS
        ],
        in_specs=[pl.BlockSpec(memory_space=pltpu.SMEM)] + [pl.BlockSpec(memory_space=pl.ANY)] * 4,
        out_specs=[pl.BlockSpec(memory_space=pltpu.VMEM)] * len(CHUNKS),
        scratch_shapes=[pltpu.SemaphoreType.DMA((4 * HEAD_HALF,))],
        name="pack_pairs",
        compiler_params=pltpu.CompilerParams(vmem_limit_bytes=VMEM_MIB * 2**20),
        cost_estimate=pl.CostEstimate(flops=0, bytes_accessed=2**20, transcendentals=0),
    )(where, PIN(keys), PIN(values), keys_other, values_other)


def attend_kernel(
    where_ref,
    rand_ref,
    q_ref,
    do_ref,
    qo_ref,
    doo_ref,
    pair_ref,
    near_ref,
    far_ref,
    corner_ref,
    dq_ref,
    dqo_ref,
    own_out,
    near_out,
    far_out,
    corner_out,
    s_ref,
    dp_ref,
    q_rows,
    do_rows,
    k_rows,
    v_rows,
    dk_ref,
    dv_ref,
):
    scale = HEAD_DIM ** (-0.5)
    factor = scale * LOG2E
    half = where_ref[0]
    me = where_ref[1]
    near = 4 - 3 * half
    far = 1 + 3 * half
    deltas = (0, near, far, near ^ far)
    outs = (own_out, near_out, far_out, corner_out)
    dq_outs = (dq_ref, dqo_ref)
    rows = GROUP * BLOCK
    unit = rows // 2
    units = 2 * rows // unit
    span = 4 * BLOCK
    spans = PART * BLOCK // span
    last = (((1,), (1,)), ((), ()))
    plain = (((1,), (0,)), ((), ()))
    first = (((0,), (0,)), ((), ()))
    dot = partial(lax.dot_general, preferred_element_type=jnp.float32)

    for b, (q, do) in enumerate(((q_ref, do_ref), (qo_ref, doo_ref))):
        for g in range(GROUP):
            at = slice(b * rows + g * BLOCK, b * rows + (g + 1) * BLOCK)
            q_rows[at, :] = q[:, g * HEAD_DIM : (g + 1) * HEAD_DIM]
            do_rows[at, :] = do[:, g * HEAD_DIM : (g + 1) * HEAD_DIM]
    for place, source in enumerate((pair_ref, near_ref, far_ref, corner_ref)):
        at = slice(place * PAIR, (place + 1) * PAIR)
        k_rows[at, :] = source[:, 0:HEAD_DIM]
        v_rows[at, :] = source[:, HEAD_DIM : 2 * HEAD_DIM]

    def count_of(b, slot):
        block = me ^ (SWAP * b)
        listed = me ^ deltas[slot // 2] ^ (SWAP * (slot % 2))
        total = (listed < GLOBALS).astype(jnp.int32)
        for w in range(WINDOW):
            total += (lax.rem(block + (w - WINDOW // 2 + PART), PART) == listed).astype(jnp.int32)
        for r in range(RANDOMS):
            total += (rand_ref[block * RANDOMS + r] == listed).astype(jnp.int32)
        return total

    counts = [[count_of(b, slot) for slot in range(PART)] for b in range(2)]

    def slots_of(u, n):
        for i in range(span // BLOCK):
            slot = n * (span // BLOCK) + i
            yield i, slice(slot * BLOCK, (slot + 1) * BLOCK), counts[u * unit // rows][slot]

    def fold(x, op):
        return op(x.reshape(BLOCK // 8, 8, unit), axis=0)

    def cols_of(u):
        return slice(u * unit, (u + 1) * unit)

    def span_of(n):
        return slice(n * span, (n + 1) * span)

    top, sums, inverse, dq = [None] * units, [None] * units, [None] * units, [None] * units

    def score(u, n):
        s = dot(k_rows[span_of(n), :], q_rows[cols_of(u), :], last)
        s_ref[span_of(n), cols_of(u)] = s
        for i, _, count in slots_of(u, n):
            part = fold(s[i * BLOCK : (i + 1) * BLOCK], jnp.max)
            part = jnp.where(count > 0, part, -1e30)
            top[u] = part if top[u] is None else jnp.maximum(top[u], part)
        if n == spans - 1:
            top[u] = jnp.max(top[u], axis=0, keepdims=True) * factor

    def soften(u, n):
        dp = dot(v_rows[span_of(n), :], do_rows[cols_of(u), :], last)
        dp_ref[span_of(n), cols_of(u)] = dp
        for i, at, count in slots_of(u, n):
            e = jnp.exp2(s_ref[at, cols_of(u)] * factor - jnp.where(count > 0, top[u], 1e30))
            s_ref[at, cols_of(u)] = e
            weight = count.astype(jnp.float32)
            total = weight * fold(e, jnp.sum)
            delta = weight * fold(e * dp[i * BLOCK : (i + 1) * BLOCK], jnp.sum)
            sums[u] = (total, delta) if sums[u] is None else (sums[u][0] + total, sums[u][1] + delta)
        if n == spans - 1:
            inverse[u] = 1.0 / jnp.sum(sums[u][0], axis=0, keepdims=True)
            sums[u] = jnp.sum(sums[u][1], axis=0, keepdims=True) * inverse[u]

    def grads(u, n):
        probs, scores = [], []
        for _, at, count in slots_of(u, n):
            p = s_ref[at, cols_of(u)] * (count.astype(jnp.float32) * inverse[u])
            probs.append(p.astype(jnp.bfloat16))
            scores.append((p * (dp_ref[at, cols_of(u)] - sums[u])).astype(jnp.bfloat16))
        probs = jnp.concatenate(probs, axis=0)
        scores = jnp.concatenate(scores, axis=0)
        dv = dot(probs, do_rows[cols_of(u), :], plain)
        dk = dot(scores, q_rows[cols_of(u), :], plain)
        if u > 0:
            dv = dv + dv_ref[span_of(n), :]
            dk = dk + dk_ref[span_of(n), :]
        if u < units - 1:
            dv_ref[span_of(n), :] = dv
            dk_ref[span_of(n), :] = dk
        else:
            dk = dk * scale
            for place in range(span // PAIR):
                out = outs[n * (span // PAIR) + place]
                at = slice(place * PAIR, (place + 1) * PAIR)
                out[:, 0:HEAD_DIM] = dk[at].astype(out.dtype)
                out[:, HEAD_DIM : 2 * HEAD_DIM] = dv[at].astype(out.dtype)
        term = dot(k_rows[span_of(n), :], scores, first)
        dq[u] = term if dq[u] is None else dq[u] + term
        if n == spans - 1:
            out = (dq[u] * scale).T.astype(jnp.bfloat16)
            for i in range(unit // BLOCK):
                b, g = divmod(u * unit // BLOCK + i, GROUP)
                dq_outs[b][:, g * HEAD_DIM : (g + 1) * HEAD_DIM] = out[i * BLOCK : (i + 1) * BLOCK]

    stages = (score, soften, grads)
    for t in range(units + len(stages) - 1):
        for n in range(spans):
            for k, stage in enumerate(stages):
                if 0 <= t - k < units:
                    stage(t - k, n)


def attend(chunk, where, rand, queries, d_out, queries_other, dout_other, sources):
    heads = CHUNKS[chunk]
    qw = GROUP * HEAD_DIM
    kw = 2 * HEAD_DIM
    first = sum(CHUNKS[:chunk])
    q_spec = pl.BlockSpec((BLOCK, qw), lambda j, w, r: (0, w[0] * HEAD_HALF + first + j))
    kv_spec = pl.BlockSpec((PAIR, kw), lambda j, w, r: (0, j))
    dq_spec = pl.BlockSpec((BLOCK, qw), lambda j, w, r: (0, j))
    rows = GROUP * BLOCK
    pairs = 2 * heads * rows * PART * BLOCK
    dq_shape = jax.ShapeDtypeStruct((BLOCK, heads * qw), jnp.bfloat16)
    wide = jax.ShapeDtypeStruct((PAIR, heads * kw), jnp.float32)
    narrow = jax.ShapeDtypeStruct((PAIR, heads * kw), jnp.bfloat16)
    return pl.pallas_call(
        attend_kernel,
        out_shape=[OUT(dq_shape), OUT(dq_shape), wide, narrow, narrow, narrow],
        grid_spec=pltpu.PrefetchScalarGridSpec(
            num_scalar_prefetch=2,
            grid=(heads,),
            in_specs=[q_spec] * 4 + [kv_spec] * 4,
            out_specs=[dq_spec] * 2 + [kv_spec] * 4,
            scratch_shapes=[
                pltpu.VMEM((PART * BLOCK, 2 * rows), jnp.float32),
                pltpu.VMEM((PART * BLOCK, 2 * rows), jnp.float32),
                pltpu.VMEM((2 * rows, HEAD_DIM), jnp.bfloat16),
                pltpu.VMEM((2 * rows, HEAD_DIM), jnp.bfloat16),
                pltpu.VMEM((PART * BLOCK, HEAD_DIM), jnp.bfloat16),
                pltpu.VMEM((PART * BLOCK, HEAD_DIM), jnp.bfloat16),
                pltpu.VMEM((PART * BLOCK, HEAD_DIM), jnp.float32),
                pltpu.VMEM((PART * BLOCK, HEAD_DIM), jnp.float32),
            ],
        ),
        name="attend",
        compiler_params=pltpu.CompilerParams(vmem_limit_bytes=VMEM_MIB * 2**20),
        cost_estimate=pl.CostEstimate(
            flops=10 * pairs * HEAD_DIM * 2, bytes_accessed=4 * 2**20, transcendentals=pairs
        ),
    )(where, rand, *map(PIN, (queries, d_out, queries_other, dout_other)), *map(PIN2, sources))


def place_kernel(columns, where_ref, *refs):
    inputs = refs[: len(columns) * 2]
    outs, sems = refs[len(columns) * 2 : -1], refs[-1]
    copies = []
    for i, pieces in enumerate(columns):
        for half in range(2):
            place = where_ref[0] ^ half
            for out, at, start, width in pieces:
                at = at + place * (outs[out].shape[1] // 2)
                source = inputs[2 * i + half].at[:, start : start + width]
                to = outs[out].at[:, lanes(at, width)]
                copies.append(pltpu.make_async_copy(source, to, sems.at[len(copies)]))
    move_all(copies)


def place(columns, where, inputs, widths, name):
    count = 2 * sum(len(pieces) for pieces in columns)
    return pl.pallas_call(
        partial(place_kernel, columns),
        out_shape=[jax.ShapeDtypeStruct((BLOCK, width), jnp.bfloat16) for width in widths],
        in_specs=[pl.BlockSpec(memory_space=pltpu.SMEM)]
        + [pl.BlockSpec(memory_space=pl.ANY)] * len(inputs),
        out_specs=[pl.BlockSpec(memory_space=pltpu.VMEM)] * len(widths),
        scratch_shapes=[pltpu.SemaphoreType.DMA((count,))],
        name=name,
        cost_estimate=pl.CostEstimate(flops=0, bytes_accessed=2**20, transcendentals=0),
    )(where, *inputs)


def place_queries(where, own, got):
    columns, inputs = [], []
    for chunk, heads in enumerate(CHUNKS):
        width = heads * GROUP * HEAD_DIM
        columns.append([(0, sum(CHUNKS[:chunk]) * GROUP * HEAD_DIM, 0, width)])
        inputs += [own[chunk], got[chunk]]
    return place(columns, where, inputs, [2 * HALF_Q], "place_queries")[0]


def place_pairs(where, own, got):
    columns, inputs = [], []
    for chunk, heads in enumerate(CHUNKS):
        pieces = []
        for head in range(heads):
            at = (sum(CHUNKS[:chunk]) + head) * HEAD_DIM
            for side in range(2):
                pieces.append((side, at, (2 * head + side) * HEAD_DIM, HEAD_DIM))
        columns.append(pieces)
        inputs += [own[chunk], got[chunk]]
    return place(columns, where, inputs, [2 * HALF_KV] * 2, "place_pairs")


def per_device_dense(queries, keys, values, d_out, rand_blocks):
    me = lax.axis_index("ctx") * 2 + lax.axis_index("uly")
    half = lax.axis_index("ctx") % 2
    where = jnp.stack([half, me]).astype(jnp.int32)
    rand = rand_blocks.reshape(PART * RANDOMS)
    keys_other = send(keys, SWAP_PERM)
    values_other = send(values, SWAP_PERM)
    pairs = pack_pairs(where, keys, values, keys_other, values_other)
    queries, d_out, pairs = lax.optimization_barrier((queries, d_out, pairs))
    queries_other = send(queries, SWAP_PERM)
    dout_other = send(d_out, SWAP_PERM)
    nears = [send(pair, NEAR_PERM) for pair in pairs]
    fars = [send(pair, FAR_PERM) for pair in pairs]
    corners = [send(near, FAR_PERM) for near in nears]
    terms, dq_own, dq_got = [], [], []
    for chunk in range(len(CHUNKS)):
        dq_mine, dq_other, own_grads, near_grads, far_grads, corner_grads = attend(
            chunk,
            where,
            rand,
            queries,
            d_out,
            queries_other,
            dout_other,
            (pairs[chunk], nears[chunk], fars[chunk], corners[chunk]),
        )
        arrived = [send(corner_grads, CORNER_PERM), send(near_grads, NEAR_PERM)]
        if terms:
            far_grads, terms[-1] = lax.optimization_barrier((far_grads, terms[-1]))
        arrived.append(send(far_grads, FAR_PERM))
        terms.append((own_grads, arrived))
        dq_own.append(dq_mine)
        dq_got.append(send(dq_other, SWAP_PERM))
    d_queries = place_queries(where, dq_own, dq_got)

    own, other = [], []
    for own_grads, arrived in terms:
        mine, theirs = (
            sum((x[at].astype(jnp.float32) for x in arrived), own_grads[at]).astype(jnp.bfloat16)
            for at in (slice(0, BLOCK), slice(BLOCK, PAIR))
        )
        own.append(mine)
        other.append(send(theirs, SWAP_PERM))
    first = half == 0
    d_keys, d_values = (
        jnp.concatenate(
            [
                jnp.where(first == (side == 0), mine[:, at : at + HEAD_DIM], got[:, at : at + HEAD_DIM])
                for side in range(2)
                for mine, got in zip(own, other)
                for at in range(place * HEAD_DIM, mine.shape[1], 2 * HEAD_DIM)
            ],
            axis=1,
        )
        for place in range(2)
    )
    return (d_queries, d_keys, d_values)


def per_device(queries, keys, values, d_out, rand_blocks):
    dense = (
        lax.axis_size("ctx") == 4
        and lax.axis_size("uly") == 2
        and rand_blocks.shape[0] == PART
        and keys.shape == (BLOCK, 2 * HALF_KV)
    )
    plan = per_device_dense if dense else per_device_sparse
    return plan(queries, keys, values, d_out, rand_blocks)


def solution(mesh):
    in_specs = (
        P(("dp", "ctx", "uly"), None),
        P(("dp", "ctx", "uly"), None),
        P(("dp", "ctx", "uly"), None),
        P(("dp", "ctx", "uly"), None),
        P("dp", None),
    )
    out_specs = (
        P(("dp", "ctx", "uly"), None),
        P(("dp", "ctx", "uly"), None),
        P(("dp", "ctx", "uly"), None),
    )
    return jax.shard_map(
        per_device, mesh=mesh, in_specs=in_specs, out_specs=out_specs, check_vma=False
    )
```

```python
from functools import partial

import jax
import jax.numpy as jnp
from jax import lax
from jax.experimental import pallas as pl
from jax.experimental.pallas import tpu as pltpu
from jax.sharding import PartitionSpec as P

HEAD_DIM = 128
BLOCK = 128
WINDOW = 3
GLOBALS = 2
RANDOMS = 3
ENTRIES = 8
GROUP = 4


def listed_blocks(rand_blocks):
    total = rand_blocks.shape[0]
    block_ids = jnp.arange(total, dtype=jnp.int32)
    window_part = (
        block_ids[:, None] + jnp.arange(WINDOW, dtype=jnp.int32)[None, :] - WINDOW // 2
    ) % total
    global_part = jnp.broadcast_to(jnp.arange(GLOBALS, dtype=jnp.int32)[None, :], (total, GLOBALS))
    return jnp.concatenate([window_part, global_part, rand_blocks], axis=1)


def block_backward(sources, softmax_scale, inputs):
    query_blk, dout_blk, source_rows = inputs
    picked = jnp.take(sources, source_rows, axis=0)
    kv_width = picked.shape[-1] // 2
    kv_count = kv_width // HEAD_DIM
    key_sel = picked[..., :kv_width].reshape(ENTRIES, BLOCK, kv_count, HEAD_DIM)
    value_sel = picked[..., kv_width:].reshape(ENTRIES, BLOCK, kv_count, HEAD_DIM)
    query_four = query_blk.reshape(BLOCK, kv_count, GROUP, HEAD_DIM)
    dout_four = dout_blk.reshape(BLOCK, kv_count, GROUP, HEAD_DIM)
    scores = jnp.einsum("tkgd,eskd->kgtes", query_four, key_sel, preferred_element_type=jnp.float32)
    scores = scores.reshape(kv_count, GROUP, BLOCK, ENTRIES * BLOCK) * softmax_scale
    row_max = jnp.max(scores, axis=-1, keepdims=True)
    exp_scores = jnp.exp(scores - row_max)
    prob_rows = exp_scores / jnp.sum(exp_scores, axis=-1, keepdims=True)
    grad_probs = jnp.einsum(
        "tkgd,eskd->kgtes", dout_four, value_sel, preferred_element_type=jnp.float32
    )
    grad_probs = grad_probs.reshape(kv_count, GROUP, BLOCK, ENTRIES * BLOCK)
    row_delta = jnp.sum(prob_rows * grad_probs, axis=-1, keepdims=True)
    grad_scores = (
        (prob_rows * (grad_probs - row_delta))
        .astype(jnp.bfloat16)
        .reshape(kv_count, GROUP, BLOCK, ENTRIES, BLOCK)
    )
    probs_low = prob_rows.astype(jnp.bfloat16).reshape(kv_count, GROUP, BLOCK, ENTRIES, BLOCK)
    grad_values = jnp.einsum(
        "kgtes,tkgd->eskd", probs_low, dout_four, preferred_element_type=jnp.float32
    )
    grad_keys = (
        jnp.einsum("kgtes,tkgd->eskd", grad_scores, query_four, preferred_element_type=jnp.float32)
        * softmax_scale
    )
    grad_query = (
        jnp.einsum("kgtes,eskd->tkgd", grad_scores, key_sel, preferred_element_type=jnp.float32)
        * softmax_scale
    )
    partials = jnp.concatenate(
        [
            grad_keys.reshape(ENTRIES, BLOCK, kv_width),
            grad_values.reshape(ENTRIES, BLOCK, kv_width),
        ],
        axis=-1,
    )
    return (partials, grad_query.reshape(BLOCK, kv_count * GROUP * HEAD_DIM))


def per_device_sparse(queries, keys, values, d_out, rand_blocks):
    softmax_scale = HEAD_DIM ** (-0.5)
    groups = lax.axis_size("ctx")
    my_group = lax.axis_index("ctx")
    queries_here, dout_here, keys_here, values_here = (
        lax.all_to_all(queries, "uly", split_axis=1, concat_axis=0, tiled=True),
        lax.all_to_all(d_out, "uly", split_axis=1, concat_axis=0, tiled=True),
        lax.all_to_all(keys, "uly", split_axis=1, concat_axis=0, tiled=True),
        lax.all_to_all(values, "uly", split_axis=1, concat_axis=0, tiled=True),
    )
    tokens_here = keys_here.shape[0]
    per_group = tokens_here // BLOCK
    kv_width = keys_here.shape[1]
    local_blocks = jnp.concatenate([keys_here, values_here], axis=1).reshape(
        per_group, BLOCK, 2 * kv_width
    )
    listed = listed_blocks(rand_blocks)
    owners = listed // per_group
    offsets = listed % per_group
    requester = (jnp.arange(listed.shape[0], dtype=jnp.int32) // per_group)[:, None]
    entry_ids = jnp.arange(ENTRIES, dtype=jnp.int32)
    is_global = (entry_ids >= WINDOW) & (entry_ids < WINDOW + GLOBALS)
    entry_global = jnp.tile(is_global, per_group)
    global_slot = jnp.tile(entry_ids - WINDOW, per_group)
    rand_capacity = per_group * RANDOMS // groups + 1
    remote = owners != requester
    capacity = rand_capacity + GLOBALS
    lead_slots = GLOBALS
    owners = owners.reshape(groups, per_group * ENTRIES)
    offsets = offsets.reshape(groups, per_group * ENTRIES)
    remote = remote.reshape(groups, per_group * ENTRIES)
    counted = remote & jnp.logical_not(entry_global)[None, :]
    owner_hot = (
        (owners[:, :, None] == jnp.arange(groups, dtype=jnp.int32)[None, None, :])
        & counted[:, :, None]
    ).astype(jnp.int32)
    rand_slot = jnp.sum((jnp.cumsum(owner_hot, axis=1) - 1) * owner_hot, axis=2) + lead_slots
    slot_index = jnp.where(entry_global[None, :], global_slot[None, :], rand_slot)
    for_me = remote & (owners == my_group)
    slot_match = (
        slot_index[:, :, None, None] == jnp.arange(capacity, dtype=jnp.int32)[None, None, :, None]
    )
    block_match = (
        offsets[:, :, None, None] == jnp.arange(per_group, dtype=jnp.int32)[None, None, None, :]
    )
    slot_picker = jnp.minimum(
        jnp.sum((for_me[:, :, None, None] & slot_match & block_match).astype(jnp.int32), axis=1), 1
    )
    outgoing = jnp.einsum(
        "csb,bxd->csxd",
        slot_picker.astype(jnp.bfloat16),
        local_blocks,
        preferred_element_type=jnp.float32,
    ).astype(jnp.bfloat16)
    incoming = lax.all_to_all(outgoing, "ctx", split_axis=0, concat_axis=0, tiled=True)
    my_owner = lax.dynamic_index_in_dim(owners, my_group, 0, keepdims=False)
    my_slot = lax.dynamic_index_in_dim(slot_index, my_group, 0, keepdims=False)
    my_offset = lax.dynamic_index_in_dim(offsets, my_group, 0, keepdims=False)
    my_remote = lax.dynamic_index_in_dim(remote, my_group, 0, keepdims=False)
    source_rows = jnp.where(my_remote, per_group + my_owner * capacity + my_slot, my_offset)
    pieces = [local_blocks, incoming.reshape(groups * capacity, BLOCK, 2 * kv_width)]
    sources = jnp.concatenate(pieces, axis=0)
    source_count = sources.shape[0]
    query_blocks = queries_here.reshape(per_group, BLOCK, queries_here.shape[1])
    dout_blocks = dout_here.reshape(per_group, BLOCK, dout_here.shape[1])
    partials, grad_query = lax.map(
        partial(block_backward, sources, softmax_scale),
        (query_blocks, dout_blocks, source_rows.reshape(per_group, ENTRIES)),
    )
    source_hot = (
        source_rows[:, None] == jnp.arange(source_count, dtype=jnp.int32)[None, :]
    ).astype(jnp.float32)
    source_grads = jnp.einsum(
        "ms,mxd->sxd",
        source_hot,
        partials.reshape(per_group * ENTRIES, BLOCK, 2 * kv_width),
        precision=lax.Precision.HIGHEST,
    )
    own_grads = source_grads[:per_group]
    sent_grads = source_grads[per_group : per_group + groups * capacity].reshape(
        groups, capacity, BLOCK, 2 * kv_width
    )
    returned = lax.all_to_all(sent_grads, "ctx", split_axis=0, concat_axis=0, tiled=True)
    own_grads = own_grads + jnp.einsum(
        "csb,csxd->bxd", slot_picker.astype(jnp.float32), returned, precision=lax.Precision.HIGHEST
    )
    query_grads = grad_query.reshape(tokens_here, queries_here.shape[1]).astype(jnp.bfloat16)
    key_grads = own_grads[..., :kv_width].reshape(tokens_here, kv_width).astype(jnp.bfloat16)
    value_grads = own_grads[..., kv_width:].reshape(tokens_here, kv_width).astype(jnp.bfloat16)
    d_queries, d_keys, d_values = (
        lax.all_to_all(query_grads, "uly", split_axis=0, concat_axis=1, tiled=True),
        lax.all_to_all(key_grads, "uly", split_axis=0, concat_axis=1, tiled=True),
        lax.all_to_all(value_grads, "uly", split_axis=0, concat_axis=1, tiled=True),
    )
    return (d_queries, d_keys, d_values)


LOG2E = 1.4426950408889634
PART = 8
HEAD_HALF = 4
CHUNKS = (2, 2)
RELAY = (False, True)
VMEM_MIB = 48
PIN2 = PIN3 = lambda x: x
OUT = lambda x: x
PIN = partial(pltpu.with_memory_space_constraint, memory_space=pltpu.HBM)
HALF_Q = HEAD_HALF * GROUP * HEAD_DIM
HALF_KV = HEAD_HALF * HEAD_DIM
PAIR = 2 * BLOCK
AXES = ("ctx", "uly")

SWAP = 2


def perm_to(first, second):
    return [(i, i ^ (second if i & SWAP else first)) for i in range(PART)]


SWAP_PERM = perm_to(SWAP, SWAP)
CORNER_PERM = perm_to(5, 5)
NEAR_PERM = perm_to(4, 1)
FAR_PERM = perm_to(1, 4)


def send(array, perm):
    return lax.ppermute(array, AXES, perm)


def move_all(copies):
    for copy in copies:
        copy.start()
    for copy in copies:
        copy.wait()


def lanes(start, width):
    return pl.ds(pl.multiple_of(start, HEAD_DIM), width)


def pack_kernel(where_ref, k_ref, v_ref, ko_ref, vo_ref, *refs):
    outs, sems = refs[:-1], refs[-1]
    copies = []
    for chunk, heads in enumerate(CHUNKS):
        for head in range(heads):
            at = where_ref[0] * HALF_KV + (sum(CHUNKS[:chunk]) + head) * HEAD_DIM
            for row, pieces in enumerate(((k_ref, v_ref), (ko_ref, vo_ref))):
                for side, ref in enumerate(pieces):
                    to = outs[chunk].at[
                        row * BLOCK : (row + 1) * BLOCK,
                        (2 * head + side) * HEAD_DIM : (2 * head + side + 1) * HEAD_DIM,
                    ]
                    sem = sems.at[len(copies)]
                    source = ref.at[:, lanes(at, HEAD_DIM)]
                    copies.append(pltpu.make_async_copy(source, to, sem))
    move_all(copies)


def pack_pairs(where, keys, values, keys_other, values_other):
    return pl.pallas_call(
        pack_kernel,
        out_shape=[
            jax.ShapeDtypeStruct((PAIR, 2 * HEAD_DIM * heads), jnp.bfloat16) for heads in CHUNKS
        ],
        in_specs=[pl.BlockSpec(memory_space=pltpu.SMEM)] + [pl.BlockSpec(memory_space=pl.ANY)] * 4,
        out_specs=[pl.BlockSpec(memory_space=pltpu.VMEM)] * len(CHUNKS),
        scratch_shapes=[pltpu.SemaphoreType.DMA((4 * HEAD_HALF,))],
        name="pack_pairs",
        compiler_params=pltpu.CompilerParams(vmem_limit_bytes=VMEM_MIB * 2**20),
        cost_estimate=pl.CostEstimate(flops=0, bytes_accessed=2**20, transcendentals=0),
    )(where, PIN(keys), PIN(values), keys_other, values_other)


def attend_kernel(
    where_ref,
    rand_ref,
    q_ref,
    do_ref,
    qo_ref,
    doo_ref,
    pair_ref,
    near_ref,
    far_ref,
    corner_ref,
    dq_ref,
    dqo_ref,
    own_out,
    near_out,
    far_out,
    corner_out,
    s_ref,
    dp_ref,
    q_rows,
    do_rows,
    k_rows,
    v_rows,
    dk_ref,
    dv_ref,
):
    scale = HEAD_DIM ** (-0.5)
    factor = scale * LOG2E
    half = where_ref[0]
    me = where_ref[1]
    near = 4 - 3 * half
    far = 1 + 3 * half
    deltas = (0, near, far, near ^ far)
    outs = (own_out, near_out, far_out, corner_out)
    dq_outs = (dq_ref, dqo_ref)
    rows = GROUP * BLOCK
    unit = rows // 2
    units = 2 * rows // unit
    span = 4 * BLOCK
    spans = PART * BLOCK // span
    last = (((1,), (1,)), ((), ()))
    plain = (((1,), (0,)), ((), ()))
    first = (((0,), (0,)), ((), ()))
    dot = partial(lax.dot_general, preferred_element_type=jnp.float32)

    for b, (q, do) in enumerate(((q_ref, do_ref), (qo_ref, doo_ref))):
        for g in range(GROUP):
            at = slice(b * rows + g * BLOCK, b * rows + (g + 1) * BLOCK)
            q_rows[at, :] = q[:, g * HEAD_DIM : (g + 1) * HEAD_DIM]
            do_rows[at, :] = do[:, g * HEAD_DIM : (g + 1) * HEAD_DIM]
    for place, source in enumerate((pair_ref, near_ref, far_ref, corner_ref)):
        at = slice(place * PAIR, (place + 1) * PAIR)
        k_rows[at, :] = source[:, 0:HEAD_DIM]
        v_rows[at, :] = source[:, HEAD_DIM : 2 * HEAD_DIM]

    def count_of(b, slot):
        block = me ^ (SWAP * b)
        listed = me ^ deltas[slot // 2] ^ (SWAP * (slot % 2))
        total = (listed < GLOBALS).astype(jnp.int32)
        for w in range(WINDOW):
            total += (lax.rem(block + (w - WINDOW // 2 + PART), PART) == listed).astype(jnp.int32)
        for r in range(RANDOMS):
            total += (rand_ref[block * RANDOMS + r] == listed).astype(jnp.int32)
        return total

    counts = [[count_of(b, slot) for slot in range(PART)] for b in range(2)]

    def slots_of(u, n):
        for i in range(span // BLOCK):
            slot = n * (span // BLOCK) + i
            yield i, slice(slot * BLOCK, (slot + 1) * BLOCK), counts[u * unit // rows][slot]

    def fold(x, op):
        return op(x.reshape(BLOCK // 8, 8, unit), axis=0)

    def cols_of(u):
        return slice(u * unit, (u + 1) * unit)

    def span_of(n):
        return slice(n * span, (n + 1) * span)

    top, sums, inverse, dq = [None] * units, [None] * units, [None] * units, [None] * units

    def score(u, n):
        s = dot(k_rows[span_of(n), :], q_rows[cols_of(u), :], last)
        s_ref[span_of(n), cols_of(u)] = s
        for i, _, count in slots_of(u, n):
            part = fold(s[i * BLOCK : (i + 1) * BLOCK], jnp.max)
            part = jnp.where(count > 0, part, -1e30)
            top[u] = part if top[u] is None else jnp.maximum(top[u], part)
        if n == spans - 1:
            top[u] = jnp.max(top[u], axis=0, keepdims=True) * factor

    def soften(u, n):
        dp = dot(v_rows[span_of(n), :], do_rows[cols_of(u), :], last)
        dp_ref[span_of(n), cols_of(u)] = dp
        for i, at, count in slots_of(u, n):
            e = jnp.exp2(s_ref[at, cols_of(u)] * factor - jnp.where(count > 0, top[u], 1e30))
            s_ref[at, cols_of(u)] = e
            weight = count.astype(jnp.float32)
            total = weight * fold(e, jnp.sum)
            delta = weight * fold(e * dp[i * BLOCK : (i + 1) * BLOCK], jnp.sum)
            sums[u] = (total, delta) if sums[u] is None else (sums[u][0] + total, sums[u][1] + delta)
        if n == spans - 1:
            inverse[u] = 1.0 / jnp.sum(sums[u][0], axis=0, keepdims=True)
            sums[u] = jnp.sum(sums[u][1], axis=0, keepdims=True) * inverse[u]

    def grads(u, n):
        probs, scores = [], []
        for _, at, count in slots_of(u, n):
            p = s_ref[at, cols_of(u)] * (count.astype(jnp.float32) * inverse[u])
            probs.append(p.astype(jnp.bfloat16))
            scores.append((p * (dp_ref[at, cols_of(u)] - sums[u])).astype(jnp.bfloat16))
        probs = jnp.concatenate(probs, axis=0)
        scores = jnp.concatenate(scores, axis=0)
        dv = dot(probs, do_rows[cols_of(u), :], plain)
        dk = dot(scores, q_rows[cols_of(u), :], plain)
        if u > 0:
            dv = dv + dv_ref[span_of(n), :]
            dk = dk + dk_ref[span_of(n), :]
        if u < units - 1:
            dv_ref[span_of(n), :] = dv
            dk_ref[span_of(n), :] = dk
        else:
            dk = dk * scale
            for place in range(span // PAIR):
                out = outs[n * (span // PAIR) + place]
                at = slice(place * PAIR, (place + 1) * PAIR)
                out[:, 0:HEAD_DIM] = dk[at].astype(out.dtype)
                out[:, HEAD_DIM : 2 * HEAD_DIM] = dv[at].astype(out.dtype)
        term = dot(k_rows[span_of(n), :], scores, first)
        dq[u] = term if dq[u] is None else dq[u] + term
        if n == spans - 1:
            out = (dq[u] * scale).T.astype(jnp.bfloat16)
            for i in range(unit // BLOCK):
                b, g = divmod(u * unit // BLOCK + i, GROUP)
                dq_outs[b][:, g * HEAD_DIM : (g + 1) * HEAD_DIM] = out[i * BLOCK : (i + 1) * BLOCK]

    stages = (score, soften, grads)
    for t in range(units + len(stages) - 1):
        for n in range(spans):
            for k, stage in enumerate(stages):
                if 0 <= t - k < units:
                    stage(t - k, n)


def attend(chunk, where, rand, queries, d_out, queries_other, dout_other, sources):
    heads = CHUNKS[chunk]
    qw = GROUP * HEAD_DIM
    kw = 2 * HEAD_DIM
    first = sum(CHUNKS[:chunk])
    q_spec = pl.BlockSpec((BLOCK, qw), lambda j, w, r: (0, w[0] * HEAD_HALF + first + j))
    kv_spec = pl.BlockSpec((PAIR, kw), lambda j, w, r: (0, j))
    dq_spec = pl.BlockSpec((BLOCK, qw), lambda j, w, r: (0, j))
    rows = GROUP * BLOCK
    pairs = 2 * heads * rows * PART * BLOCK
    dq_shape = jax.ShapeDtypeStruct((BLOCK, heads * qw), jnp.bfloat16)
    wide = jax.ShapeDtypeStruct((PAIR, heads * kw), jnp.float32)
    narrow = jax.ShapeDtypeStruct((PAIR, heads * kw), jnp.bfloat16)
    return pl.pallas_call(
        attend_kernel,
        out_shape=[OUT(dq_shape), OUT(dq_shape), wide, wide if RELAY[chunk] else narrow, narrow, narrow],
        grid_spec=pltpu.PrefetchScalarGridSpec(
            num_scalar_prefetch=2,
            grid=(heads,),
            in_specs=[q_spec] * 4 + [kv_spec] * 4,
            out_specs=[dq_spec] * 2 + [kv_spec] * 4,
            scratch_shapes=[
                pltpu.VMEM((PART * BLOCK, 2 * rows), jnp.float32),
                pltpu.VMEM((PART * BLOCK, 2 * rows), jnp.float32),
                pltpu.VMEM((2 * rows, HEAD_DIM), jnp.bfloat16),
                pltpu.VMEM((2 * rows, HEAD_DIM), jnp.bfloat16),
                pltpu.VMEM((PART * BLOCK, HEAD_DIM), jnp.bfloat16),
                pltpu.VMEM((PART * BLOCK, HEAD_DIM), jnp.bfloat16),
                pltpu.VMEM((PART * BLOCK, HEAD_DIM), jnp.float32),
                pltpu.VMEM((PART * BLOCK, HEAD_DIM), jnp.float32),
            ],
        ),
        name="attend",
        compiler_params=pltpu.CompilerParams(vmem_limit_bytes=VMEM_MIB * 2**20),
        cost_estimate=pl.CostEstimate(
            flops=10 * pairs * HEAD_DIM * 2, bytes_accessed=4 * 2**20, transcendentals=pairs
        ),
    )(where, rand, *map(PIN, (queries, d_out, queries_other, dout_other)), *map(PIN2, sources))


def place_kernel(columns, where_ref, *refs):
    inputs = refs[: len(columns) * 2]
    outs, sems = refs[len(columns) * 2 : -1], refs[-1]
    copies = []
    for i, pieces in enumerate(columns):
        for half in range(2):
            place = where_ref[0] ^ half
            for out, at, start, width in pieces:
                at = at + place * (outs[out].shape[1] // 2)
                source = inputs[2 * i + half].at[:, start : start + width]
                to = outs[out].at[:, lanes(at, width)]
                copies.append(pltpu.make_async_copy(source, to, sems.at[len(copies)]))
    move_all(copies)


def place(columns, where, inputs, widths, name):
    count = 2 * sum(len(pieces) for pieces in columns)
    return pl.pallas_call(
        partial(place_kernel, columns),
        out_shape=[jax.ShapeDtypeStruct((BLOCK, width), jnp.bfloat16) for width in widths],
        in_specs=[pl.BlockSpec(memory_space=pltpu.SMEM)]
        + [pl.BlockSpec(memory_space=pl.ANY)] * len(inputs),
        out_specs=[pl.BlockSpec(memory_space=pltpu.VMEM)] * len(widths),
        scratch_shapes=[pltpu.SemaphoreType.DMA((count,))],
        name=name,
        cost_estimate=pl.CostEstimate(flops=0, bytes_accessed=2**20, transcendentals=0),
    )(where, *inputs)


def place_queries(where, own, got):
    columns, inputs = [], []
    for chunk, heads in enumerate(CHUNKS):
        width = heads * GROUP * HEAD_DIM
        columns.append([(0, sum(CHUNKS[:chunk]) * GROUP * HEAD_DIM, 0, width)])
        inputs += [own[chunk], got[chunk]]
    return place(columns, where, inputs, [2 * HALF_Q], "place_queries")[0]


def place_pairs(where, own, got):
    columns, inputs = [], []
    for chunk, heads in enumerate(CHUNKS):
        pieces = []
        for head in range(heads):
            at = (sum(CHUNKS[:chunk]) + head) * HEAD_DIM
            for side in range(2):
                pieces.append((side, at, (2 * head + side) * HEAD_DIM, HEAD_DIM))
        columns.append(pieces)
        inputs += [own[chunk], got[chunk]]
    return place(columns, where, inputs, [2 * HALF_KV] * 2, "place_pairs")


def per_device_dense(queries, keys, values, d_out, rand_blocks):
    me = lax.axis_index("ctx") * 2 + lax.axis_index("uly")
    half = lax.axis_index("ctx") % 2
    where = jnp.stack([half, me]).astype(jnp.int32)
    rand = rand_blocks.reshape(PART * RANDOMS)
    keys_other = send(keys, SWAP_PERM)
    values_other = send(values, SWAP_PERM)
    pairs = pack_pairs(where, keys, values, keys_other, values_other)
    queries, d_out, pairs = lax.optimization_barrier((queries, d_out, pairs))
    queries_other = send(queries, SWAP_PERM)
    dout_other = send(d_out, SWAP_PERM)
    nears = [send(pair, NEAR_PERM) for pair in pairs]
    fars = [send(pair, FAR_PERM) for pair in pairs]
    corners = [send(near, FAR_PERM) for near in nears]
    terms, dq_own, dq_got = [], [], []
    for chunk in range(len(CHUNKS)):
        dq_mine, dq_other, own_grads, near_grads, far_grads, corner_grads = attend(
            chunk,
            where,
            rand,
            queries,
            d_out,
            queries_other,
            dout_other,
            (pairs[chunk], nears[chunk], fars[chunk], corners[chunk]),
        )
        if RELAY[chunk]:
            from_corner = send(corner_grads, FAR_PERM).astype(jnp.float32)
            arrived = [send((near_grads + from_corner).astype(jnp.bfloat16), NEAR_PERM)]
        else:
            arrived = [send(corner_grads, CORNER_PERM), send(near_grads, NEAR_PERM)]
        if terms:
            far_grads, terms[-1] = lax.optimization_barrier((far_grads, terms[-1]))
        arrived.append(send(far_grads, FAR_PERM))
        terms.append((own_grads, arrived))
        dq_own.append(dq_mine)
        dq_got.append(send(dq_other, SWAP_PERM))
    d_queries = place_queries(where, dq_own, dq_got)

    own, other = [], []
    for own_grads, arrived in terms:
        mine, theirs = (
            sum((x[at].astype(jnp.float32) for x in arrived), own_grads[at]).astype(jnp.bfloat16)
            for at in (slice(0, BLOCK), slice(BLOCK, PAIR))
        )
        own.append(mine)
        other.append(send(theirs, SWAP_PERM))
    first = half == 0
    d_keys, d_values = (
        jnp.concatenate(
            [
                jnp.where(first == (side == 0), mine[:, at : at + HEAD_DIM], got[:, at : at + HEAD_DIM])
                for side in range(2)
                for mine, got in zip(own, other)
                for at in range(place * HEAD_DIM, mine.shape[1], 2 * HEAD_DIM)
            ],
            axis=1,
        )
        for place in range(2)
    )
    return (d_queries, d_keys, d_values)


def per_device(queries, keys, values, d_out, rand_blocks):
    dense = (
        lax.axis_size("ctx") == 4
        and lax.axis_size("uly") == 2
        and rand_blocks.shape[0] == PART
        and keys.shape == (BLOCK, 2 * HALF_KV)
    )
    plan = per_device_dense if dense else per_device_sparse
    return plan(queries, keys, values, d_out, rand_blocks)


def solution(mesh):
    in_specs = (
        P(("dp", "ctx", "uly"), None),
        P(("dp", "ctx", "uly"), None),
        P(("dp", "ctx", "uly"), None),
        P(("dp", "ctx", "uly"), None),
        P("dp", None),
    )
    out_specs = (
        P(("dp", "ctx", "uly"), None),
        P(("dp", "ctx", "uly"), None),
        P(("dp", "ctx", "uly"), None),
    )
    return jax.shard_map(
        per_device, mesh=mesh, in_specs=in_specs, out_specs=out_specs, check_vma=False
    )
```

```python
from functools import partial

import jax
import jax.numpy as jnp
from jax import lax
from jax.experimental import pallas as pl
from jax.experimental.pallas import tpu as pltpu
from jax.sharding import PartitionSpec as P

HEAD_DIM = 128
BLOCK = 128
WINDOW = 3
GLOBALS = 2
RANDOMS = 3
ENTRIES = 8
GROUP = 4


def listed_blocks(rand_blocks):
    total = rand_blocks.shape[0]
    block_ids = jnp.arange(total, dtype=jnp.int32)
    window_part = (
        block_ids[:, None] + jnp.arange(WINDOW, dtype=jnp.int32)[None, :] - WINDOW // 2
    ) % total
    global_part = jnp.broadcast_to(jnp.arange(GLOBALS, dtype=jnp.int32)[None, :], (total, GLOBALS))
    return jnp.concatenate([window_part, global_part, rand_blocks], axis=1)


def block_backward(sources, softmax_scale, inputs):
    query_blk, dout_blk, source_rows = inputs
    picked = jnp.take(sources, source_rows, axis=0)
    kv_width = picked.shape[-1] // 2
    kv_count = kv_width // HEAD_DIM
    key_sel = picked[..., :kv_width].reshape(ENTRIES, BLOCK, kv_count, HEAD_DIM)
    value_sel = picked[..., kv_width:].reshape(ENTRIES, BLOCK, kv_count, HEAD_DIM)
    query_four = query_blk.reshape(BLOCK, kv_count, GROUP, HEAD_DIM)
    dout_four = dout_blk.reshape(BLOCK, kv_count, GROUP, HEAD_DIM)
    scores = jnp.einsum("tkgd,eskd->kgtes", query_four, key_sel, preferred_element_type=jnp.float32)
    scores = scores.reshape(kv_count, GROUP, BLOCK, ENTRIES * BLOCK) * softmax_scale
    row_max = jnp.max(scores, axis=-1, keepdims=True)
    exp_scores = jnp.exp(scores - row_max)
    prob_rows = exp_scores / jnp.sum(exp_scores, axis=-1, keepdims=True)
    grad_probs = jnp.einsum(
        "tkgd,eskd->kgtes", dout_four, value_sel, preferred_element_type=jnp.float32
    )
    grad_probs = grad_probs.reshape(kv_count, GROUP, BLOCK, ENTRIES * BLOCK)
    row_delta = jnp.sum(prob_rows * grad_probs, axis=-1, keepdims=True)
    grad_scores = (
        (prob_rows * (grad_probs - row_delta))
        .astype(jnp.bfloat16)
        .reshape(kv_count, GROUP, BLOCK, ENTRIES, BLOCK)
    )
    probs_low = prob_rows.astype(jnp.bfloat16).reshape(kv_count, GROUP, BLOCK, ENTRIES, BLOCK)
    grad_values = jnp.einsum(
        "kgtes,tkgd->eskd", probs_low, dout_four, preferred_element_type=jnp.float32
    )
    grad_keys = (
        jnp.einsum("kgtes,tkgd->eskd", grad_scores, query_four, preferred_element_type=jnp.float32)
        * softmax_scale
    )
    grad_query = (
        jnp.einsum("kgtes,eskd->tkgd", grad_scores, key_sel, preferred_element_type=jnp.float32)
        * softmax_scale
    )
    partials = jnp.concatenate(
        [
            grad_keys.reshape(ENTRIES, BLOCK, kv_width),
            grad_values.reshape(ENTRIES, BLOCK, kv_width),
        ],
        axis=-1,
    )
    return (partials, grad_query.reshape(BLOCK, kv_count * GROUP * HEAD_DIM))


def per_device_sparse(queries, keys, values, d_out, rand_blocks):
    softmax_scale = HEAD_DIM ** (-0.5)
    groups = lax.axis_size("ctx")
    my_group = lax.axis_index("ctx")
    queries_here, dout_here, keys_here, values_here = (
        lax.all_to_all(queries, "uly", split_axis=1, concat_axis=0, tiled=True),
        lax.all_to_all(d_out, "uly", split_axis=1, concat_axis=0, tiled=True),
        lax.all_to_all(keys, "uly", split_axis=1, concat_axis=0, tiled=True),
        lax.all_to_all(values, "uly", split_axis=1, concat_axis=0, tiled=True),
    )
    tokens_here = keys_here.shape[0]
    per_group = tokens_here // BLOCK
    kv_width = keys_here.shape[1]
    local_blocks = jnp.concatenate([keys_here, values_here], axis=1).reshape(
        per_group, BLOCK, 2 * kv_width
    )
    listed = listed_blocks(rand_blocks)
    owners = listed // per_group
    offsets = listed % per_group
    requester = (jnp.arange(listed.shape[0], dtype=jnp.int32) // per_group)[:, None]
    entry_ids = jnp.arange(ENTRIES, dtype=jnp.int32)
    is_global = (entry_ids >= WINDOW) & (entry_ids < WINDOW + GLOBALS)
    entry_global = jnp.tile(is_global, per_group)
    global_slot = jnp.tile(entry_ids - WINDOW, per_group)
    rand_capacity = per_group * RANDOMS // groups + 1
    remote = owners != requester
    capacity = rand_capacity + GLOBALS
    lead_slots = GLOBALS
    owners = owners.reshape(groups, per_group * ENTRIES)
    offsets = offsets.reshape(groups, per_group * ENTRIES)
    remote = remote.reshape(groups, per_group * ENTRIES)
    counted = remote & jnp.logical_not(entry_global)[None, :]
    owner_hot = (
        (owners[:, :, None] == jnp.arange(groups, dtype=jnp.int32)[None, None, :])
        & counted[:, :, None]
    ).astype(jnp.int32)
    rand_slot = jnp.sum((jnp.cumsum(owner_hot, axis=1) - 1) * owner_hot, axis=2) + lead_slots
    slot_index = jnp.where(entry_global[None, :], global_slot[None, :], rand_slot)
    for_me = remote & (owners == my_group)
    slot_match = (
        slot_index[:, :, None, None] == jnp.arange(capacity, dtype=jnp.int32)[None, None, :, None]
    )
    block_match = (
        offsets[:, :, None, None] == jnp.arange(per_group, dtype=jnp.int32)[None, None, None, :]
    )
    slot_picker = jnp.minimum(
        jnp.sum((for_me[:, :, None, None] & slot_match & block_match).astype(jnp.int32), axis=1), 1
    )
    outgoing = jnp.einsum(
        "csb,bxd->csxd",
        slot_picker.astype(jnp.bfloat16),
        local_blocks,
        preferred_element_type=jnp.float32,
    ).astype(jnp.bfloat16)
    incoming = lax.all_to_all(outgoing, "ctx", split_axis=0, concat_axis=0, tiled=True)
    my_owner = lax.dynamic_index_in_dim(owners, my_group, 0, keepdims=False)
    my_slot = lax.dynamic_index_in_dim(slot_index, my_group, 0, keepdims=False)
    my_offset = lax.dynamic_index_in_dim(offsets, my_group, 0, keepdims=False)
    my_remote = lax.dynamic_index_in_dim(remote, my_group, 0, keepdims=False)
    source_rows = jnp.where(my_remote, per_group + my_owner * capacity + my_slot, my_offset)
    pieces = [local_blocks, incoming.reshape(groups * capacity, BLOCK, 2 * kv_width)]
    sources = jnp.concatenate(pieces, axis=0)
    source_count = sources.shape[0]
    query_blocks = queries_here.reshape(per_group, BLOCK, queries_here.shape[1])
    dout_blocks = dout_here.reshape(per_group, BLOCK, dout_here.shape[1])
    partials, grad_query = lax.map(
        partial(block_backward, sources, softmax_scale),
        (query_blocks, dout_blocks, source_rows.reshape(per_group, ENTRIES)),
    )
    source_hot = (
        source_rows[:, None] == jnp.arange(source_count, dtype=jnp.int32)[None, :]
    ).astype(jnp.float32)
    source_grads = jnp.einsum(
        "ms,mxd->sxd",
        source_hot,
        partials.reshape(per_group * ENTRIES, BLOCK, 2 * kv_width),
        precision=lax.Precision.HIGHEST,
    )
    own_grads = source_grads[:per_group]
    sent_grads = source_grads[per_group : per_group + groups * capacity].reshape(
        groups, capacity, BLOCK, 2 * kv_width
    )
    returned = lax.all_to_all(sent_grads, "ctx", split_axis=0, concat_axis=0, tiled=True)
    own_grads = own_grads + jnp.einsum(
        "csb,csxd->bxd", slot_picker.astype(jnp.float32), returned, precision=lax.Precision.HIGHEST
    )
    query_grads = grad_query.reshape(tokens_here, queries_here.shape[1]).astype(jnp.bfloat16)
    key_grads = own_grads[..., :kv_width].reshape(tokens_here, kv_width).astype(jnp.bfloat16)
    value_grads = own_grads[..., kv_width:].reshape(tokens_here, kv_width).astype(jnp.bfloat16)
    d_queries, d_keys, d_values = (
        lax.all_to_all(query_grads, "uly", split_axis=0, concat_axis=1, tiled=True),
        lax.all_to_all(key_grads, "uly", split_axis=0, concat_axis=1, tiled=True),
        lax.all_to_all(value_grads, "uly", split_axis=0, concat_axis=1, tiled=True),
    )
    return (d_queries, d_keys, d_values)


LOG2E = 1.4426950408889634
PART = 8
HEAD_HALF = 4
CHUNKS = (2, 2)
RELAY = (False, True)
VMEM_MIB = 48
PIN2 = PIN3 = lambda x: x
OUT = lambda x: x
PIN = partial(pltpu.with_memory_space_constraint, memory_space=pltpu.HBM)
HALF_Q = HEAD_HALF * GROUP * HEAD_DIM
HALF_KV = HEAD_HALF * HEAD_DIM
PAIR = 2 * BLOCK
AXES = ("ctx", "uly")

SWAP = 2


def perm_to(first, second):
    return [(i, i ^ (second if i & SWAP else first)) for i in range(PART)]


SWAP_PERM = perm_to(SWAP, SWAP)
CORNER_PERM = perm_to(5, 5)
NEAR_PERM = perm_to(4, 1)
FAR_PERM = perm_to(1, 4)


def send(array, perm):
    return lax.ppermute(array, AXES, perm)


def move_all(copies):
    for copy in copies:
        copy.start()
    for copy in copies:
        copy.wait()


def lanes(start, width):
    return pl.ds(pl.multiple_of(start, HEAD_DIM), width)


def pack_kernel(where_ref, k_ref, v_ref, ko_ref, vo_ref, *refs):
    outs, sems = refs[:-1], refs[-1]
    copies = []
    for chunk, heads in enumerate(CHUNKS):
        for head in range(heads):
            at = where_ref[0] * HALF_KV + (sum(CHUNKS[:chunk]) + head) * HEAD_DIM
            for row, pieces in enumerate(((k_ref, v_ref), (ko_ref, vo_ref))):
                for side, ref in enumerate(pieces):
                    to = outs[chunk].at[
                        row * BLOCK : (row + 1) * BLOCK,
                        (2 * head + side) * HEAD_DIM : (2 * head + side + 1) * HEAD_DIM,
                    ]
                    sem = sems.at[len(copies)]
                    source = ref.at[:, lanes(at, HEAD_DIM)]
                    copies.append(pltpu.make_async_copy(source, to, sem))
    move_all(copies)


def pack_pairs(where, keys, values, keys_other, values_other):
    return pl.pallas_call(
        pack_kernel,
        out_shape=[
            jax.ShapeDtypeStruct((PAIR, 2 * HEAD_DIM * heads), jnp.bfloat16) for heads in CHUNKS
        ],
        in_specs=[pl.BlockSpec(memory_space=pltpu.SMEM)] + [pl.BlockSpec(memory_space=pl.ANY)] * 4,
        out_specs=[pl.BlockSpec(memory_space=pltpu.VMEM)] * len(CHUNKS),
        scratch_shapes=[pltpu.SemaphoreType.DMA((4 * HEAD_HALF,))],
        name="pack_pairs",
        compiler_params=pltpu.CompilerParams(vmem_limit_bytes=VMEM_MIB * 2**20),
        cost_estimate=pl.CostEstimate(flops=0, bytes_accessed=2**20, transcendentals=0),
    )(where, PIN(keys), PIN(values), keys_other, values_other)


def attend_kernel(
    where_ref,
    rand_ref,
    q_ref,
    do_ref,
    qo_ref,
    doo_ref,
    pair_ref,
    near_ref,
    far_ref,
    corner_ref,
    dq_ref,
    dqo_ref,
    own_out,
    near_out,
    far_out,
    corner_out,
    s_ref,
    dp_ref,
    q_rows,
    do_rows,
    k_rows,
    v_rows,
    dk_ref,
    dv_ref,
):
    scale = HEAD_DIM ** (-0.5)
    factor = scale * LOG2E
    half = where_ref[0]
    me = where_ref[1]
    near = 4 - 3 * half
    far = 1 + 3 * half
    deltas = (0, near, far, near ^ far)
    outs = (own_out, near_out, far_out, corner_out)
    dq_outs = (dq_ref, dqo_ref)
    rows = GROUP * BLOCK
    unit = rows // 2
    units = 2 * rows // unit
    span = 4 * BLOCK
    spans = PART * BLOCK // span
    last = (((1,), (1,)), ((), ()))
    plain = (((1,), (0,)), ((), ()))
    first = (((0,), (0,)), ((), ()))
    dot = partial(lax.dot_general, preferred_element_type=jnp.float32)

    for b, (q, do) in enumerate(((q_ref, do_ref), (qo_ref, doo_ref))):
        for g in range(GROUP):
            at = slice(b * rows + g * BLOCK, b * rows + (g + 1) * BLOCK)
            q_rows[at, :] = q[:, g * HEAD_DIM : (g + 1) * HEAD_DIM]
            do_rows[at, :] = do[:, g * HEAD_DIM : (g + 1) * HEAD_DIM]
    for place, source in enumerate((pair_ref, near_ref, far_ref, corner_ref)):
        at = slice(place * PAIR, (place + 1) * PAIR)
        k_rows[at, :] = source[:, 0:HEAD_DIM]
        v_rows[at, :] = source[:, HEAD_DIM : 2 * HEAD_DIM]

    def count_of(b, slot):
        block = me ^ (SWAP * b)
        listed = me ^ deltas[slot // 2] ^ (SWAP * (slot % 2))
        total = (listed < GLOBALS).astype(jnp.int32)
        for w in range(WINDOW):
            total += (lax.rem(block + (w - WINDOW // 2 + PART), PART) == listed).astype(jnp.int32)
        for r in range(RANDOMS):
            total += (rand_ref[block * RANDOMS + r] == listed).astype(jnp.int32)
        return total

    counts = [[count_of(b, slot) for slot in range(PART)] for b in range(2)]

    def slots_of(u, n):
        for i in range(span // BLOCK):
            slot = n * (span // BLOCK) + i
            yield i, slice(slot * BLOCK, (slot + 1) * BLOCK), counts[u * unit // rows][slot]

    def fold(x, op):
        return op(x.reshape(BLOCK // 8, 8, unit), axis=0)

    def cols_of(u):
        return slice(u * unit, (u + 1) * unit)

    def span_of(n):
        return slice(n * span, (n + 1) * span)

    top, sums, inverse, dq = [None] * units, [None] * units, [None] * units, [None] * units

    def score(u, n):
        s = dot(k_rows[span_of(n), :], q_rows[cols_of(u), :], last)
        s_ref[span_of(n), cols_of(u)] = s
        for i, _, count in slots_of(u, n):
            part = fold(s[i * BLOCK : (i + 1) * BLOCK], jnp.max)
            part = jnp.where(count > 0, part, -1e30)
            top[u] = part if top[u] is None else jnp.maximum(top[u], part)
        if n == spans - 1:
            top[u] = jnp.max(top[u], axis=0, keepdims=True) * factor

    def soften(u, n):
        dp = dot(v_rows[span_of(n), :], do_rows[cols_of(u), :], last)
        dp_ref[span_of(n), cols_of(u)] = dp
        for i, at, count in slots_of(u, n):
            e = jnp.exp2(s_ref[at, cols_of(u)] * factor - jnp.where(count > 0, top[u], 1e30))
            s_ref[at, cols_of(u)] = e
            weight = count.astype(jnp.float32)
            total = weight * fold(e, jnp.sum)
            delta = weight * fold(e * dp[i * BLOCK : (i + 1) * BLOCK], jnp.sum)
            sums[u] = (total, delta) if sums[u] is None else (sums[u][0] + total, sums[u][1] + delta)
        if n == spans - 1:
            inverse[u] = 1.0 / jnp.sum(sums[u][0], axis=0, keepdims=True)
            sums[u] = jnp.sum(sums[u][1], axis=0, keepdims=True) * inverse[u]

    def grads(u, n):
        probs, scores = [], []
        for _, at, count in slots_of(u, n):
            p = s_ref[at, cols_of(u)] * (count.astype(jnp.float32) * inverse[u])
            probs.append(p.astype(jnp.bfloat16))
            scores.append((p * (dp_ref[at, cols_of(u)] - sums[u])).astype(jnp.bfloat16))
        probs = jnp.concatenate(probs, axis=0)
        scores = jnp.concatenate(scores, axis=0)
        dv = dot(probs, do_rows[cols_of(u), :], plain)
        dk = dot(scores, q_rows[cols_of(u), :], plain)
        if u > 0:
            dv = dv + dv_ref[span_of(n), :]
            dk = dk + dk_ref[span_of(n), :]
        if u < units - 1:
            dv_ref[span_of(n), :] = dv
            dk_ref[span_of(n), :] = dk
        else:
            dk = dk * scale
            for place in range(span // PAIR):
                out = outs[n * (span // PAIR) + place]
                at = slice(place * PAIR, (place + 1) * PAIR)
                out[:, 0:HEAD_DIM] = dk[at].astype(out.dtype)
                out[:, HEAD_DIM : 2 * HEAD_DIM] = dv[at].astype(out.dtype)
        term = dot(k_rows[span_of(n), :], scores, first)
        dq[u] = term if dq[u] is None else dq[u] + term
        if n == spans - 1:
            out = (dq[u] * scale).T.astype(jnp.bfloat16)
            for i in range(unit // BLOCK):
                b, g = divmod(u * unit // BLOCK + i, GROUP)
                dq_outs[b][:, g * HEAD_DIM : (g + 1) * HEAD_DIM] = out[i * BLOCK : (i + 1) * BLOCK]

    stages = (score, soften, grads)
    for t in range(units + len(stages) - 1):
        for n in range(spans):
            for k, stage in enumerate(stages):
                if 0 <= t - k < units:
                    stage(t - k, n)


def attend(chunk, where, rand, queries, d_out, queries_other, dout_other, sources):
    heads = CHUNKS[chunk]
    qw = GROUP * HEAD_DIM
    kw = 2 * HEAD_DIM
    first = sum(CHUNKS[:chunk])
    q_spec = pl.BlockSpec((BLOCK, qw), lambda j, w, r: (0, w[0] * HEAD_HALF + first + j))
    kv_spec = pl.BlockSpec((PAIR, kw), lambda j, w, r: (0, j))
    dq_spec = pl.BlockSpec((BLOCK, qw), lambda j, w, r: (0, j))
    rows = GROUP * BLOCK
    pairs = 2 * heads * rows * PART * BLOCK
    dq_shape = jax.ShapeDtypeStruct((BLOCK, heads * qw), jnp.bfloat16)
    wide = jax.ShapeDtypeStruct((PAIR, heads * kw), jnp.float32)
    narrow = jax.ShapeDtypeStruct((PAIR, heads * kw), jnp.bfloat16)
    return pl.pallas_call(
        attend_kernel,
        out_shape=[OUT(dq_shape), OUT(dq_shape), wide, wide if RELAY[chunk] else narrow, narrow, narrow],
        grid_spec=pltpu.PrefetchScalarGridSpec(
            num_scalar_prefetch=2,
            grid=(heads,),
            in_specs=[q_spec] * 4 + [kv_spec] * 4,
            out_specs=[dq_spec] * 2 + [kv_spec] * 4,
            scratch_shapes=[
                pltpu.VMEM((PART * BLOCK, 2 * rows), jnp.float32),
                pltpu.VMEM((PART * BLOCK, 2 * rows), jnp.float32),
                pltpu.VMEM((2 * rows, HEAD_DIM), jnp.bfloat16),
                pltpu.VMEM((2 * rows, HEAD_DIM), jnp.bfloat16),
                pltpu.VMEM((PART * BLOCK, HEAD_DIM), jnp.bfloat16),
                pltpu.VMEM((PART * BLOCK, HEAD_DIM), jnp.bfloat16),
                pltpu.VMEM((PART * BLOCK, HEAD_DIM), jnp.float32),
                pltpu.VMEM((PART * BLOCK, HEAD_DIM), jnp.float32),
            ],
        ),
        name="attend",
        compiler_params=pltpu.CompilerParams(vmem_limit_bytes=VMEM_MIB * 2**20),
        cost_estimate=pl.CostEstimate(
            flops=10 * pairs * HEAD_DIM * 2, bytes_accessed=4 * 2**20, transcendentals=pairs
        ),
    )(where, rand, *map(PIN, (queries, d_out, queries_other, dout_other)), *map(PIN2, sources))


def place_kernel(columns, where_ref, *refs):
    inputs = refs[: len(columns) * 2]
    outs, sems = refs[len(columns) * 2 : -1], refs[-1]
    copies = []
    for i, pieces in enumerate(columns):
        for half in range(2):
            place = where_ref[0] ^ half
            for out, at, start, width in pieces:
                at = at + place * (outs[out].shape[1] // 2)
                source = inputs[2 * i + half].at[:, start : start + width]
                to = outs[out].at[:, lanes(at, width)]
                copies.append(pltpu.make_async_copy(source, to, sems.at[len(copies)]))
    move_all(copies)


def place(columns, where, inputs, widths, name):
    count = 2 * sum(len(pieces) for pieces in columns)
    return pl.pallas_call(
        partial(place_kernel, columns),
        out_shape=[jax.ShapeDtypeStruct((BLOCK, width), jnp.bfloat16) for width in widths],
        in_specs=[pl.BlockSpec(memory_space=pltpu.SMEM)]
        + [pl.BlockSpec(memory_space=pl.ANY)] * len(inputs),
        out_specs=[pl.BlockSpec(memory_space=pltpu.VMEM)] * len(widths),
        scratch_shapes=[pltpu.SemaphoreType.DMA((count,))],
        name=name,
        cost_estimate=pl.CostEstimate(flops=0, bytes_accessed=2**20, transcendentals=0),
    )(where, *inputs)


def place_queries(where, own, got):
    columns, inputs = [], []
    for chunk, heads in enumerate(CHUNKS):
        width = heads * GROUP * HEAD_DIM
        columns.append([(0, sum(CHUNKS[:chunk]) * GROUP * HEAD_DIM, 0, width)])
        inputs += [own[chunk], got[chunk]]
    return place(columns, where, inputs, [2 * HALF_Q], "place_queries")[0]


def place_pairs(where, own, got):
    columns, inputs = [], []
    for chunk, heads in enumerate(CHUNKS):
        pieces = []
        for head in range(heads):
            at = (sum(CHUNKS[:chunk]) + head) * HEAD_DIM
            for side in range(2):
                pieces.append((side, at, (2 * head + side) * HEAD_DIM, HEAD_DIM))
        columns.append(pieces)
        inputs += [own[chunk], got[chunk]]
    return place(columns, where, inputs, [2 * HALF_KV] * 2, "place_pairs")


def per_device_dense(queries, keys, values, d_out, rand_blocks):
    me = lax.axis_index("ctx") * 2 + lax.axis_index("uly")
    half = lax.axis_index("ctx") % 2
    where = jnp.stack([half, me]).astype(jnp.int32)
    rand = rand_blocks.reshape(PART * RANDOMS)
    keys_other = send(keys, SWAP_PERM)
    values_other = send(values, SWAP_PERM)
    pairs = pack_pairs(where, keys, values, keys_other, values_other)
    queries, d_out, pairs = lax.optimization_barrier((queries, d_out, pairs))
    queries_other = send(queries, SWAP_PERM)
    dout_other = send(d_out, SWAP_PERM)
    nears = [send(pair, NEAR_PERM) for pair in pairs]
    fars = [send(pair, FAR_PERM) for pair in pairs]
    corners = [send(pairs[0], CORNER_PERM)] + [send(near, FAR_PERM) for near in nears[1:]]
    terms, dq_own, dq_got = [], [], []
    for chunk in range(len(CHUNKS)):
        dq_mine, dq_other, own_grads, near_grads, far_grads, corner_grads = attend(
            chunk,
            where,
            rand,
            queries,
            d_out,
            queries_other,
            dout_other,
            (pairs[chunk], nears[chunk], fars[chunk], corners[chunk]),
        )
        if RELAY[chunk]:
            from_corner = send(corner_grads, FAR_PERM).astype(jnp.float32)
            arrived = [send((near_grads + from_corner).astype(jnp.bfloat16), NEAR_PERM)]
        else:
            arrived = [send(corner_grads, CORNER_PERM), send(near_grads, NEAR_PERM)]
        if terms:
            far_grads, terms[-1] = lax.optimization_barrier((far_grads, terms[-1]))
        arrived.append(send(far_grads, FAR_PERM))
        terms.append((own_grads, arrived))
        dq_own.append(dq_mine)
        dq_got.append(send(dq_other, SWAP_PERM))
    d_queries = place_queries(where, dq_own, dq_got)

    own, other = [], []
    for own_grads, arrived in terms:
        mine, theirs = (
            sum((x[at].astype(jnp.float32) for x in arrived), own_grads[at]).astype(jnp.bfloat16)
            for at in (slice(0, BLOCK), slice(BLOCK, PAIR))
        )
        own.append(mine)
        other.append(send(theirs, SWAP_PERM))
    first = half == 0
    d_keys, d_values = (
        jnp.concatenate(
            [
                jnp.where(first == (side == 0), mine[:, at : at + HEAD_DIM], got[:, at : at + HEAD_DIM])
                for side in range(2)
                for mine, got in zip(own, other)
                for at in range(place * HEAD_DIM, mine.shape[1], 2 * HEAD_DIM)
            ],
            axis=1,
        )
        for place in range(2)
    )
    return (d_queries, d_keys, d_values)


def per_device(queries, keys, values, d_out, rand_blocks):
    dense = (
        lax.axis_size("ctx") == 4
        and lax.axis_size("uly") == 2
        and rand_blocks.shape[0] == PART
        and keys.shape == (BLOCK, 2 * HALF_KV)
    )
    plan = per_device_dense if dense else per_device_sparse
    return plan(queries, keys, values, d_out, rand_blocks)


def solution(mesh):
    in_specs = (
        P(("dp", "ctx", "uly"), None),
        P(("dp", "ctx", "uly"), None),
        P(("dp", "ctx", "uly"), None),
        P(("dp", "ctx", "uly"), None),
        P("dp", None),
    )
    out_specs = (
        P(("dp", "ctx", "uly"), None),
        P(("dp", "ctx", "uly"), None),
        P(("dp", "ctx", "uly"), None),
    )
    return jax.shard_map(
        per_device, mesh=mesh, in_specs=in_specs, out_specs=out_specs, check_vma=False
    )
```
